128 devices in a mesh: rows: 32 (over y, z, core), grp: 4 (over x).
Axes of the slice: x: 4, y: 4, z: 4, core: 2. Of those that a mesh axis runs over, the one named last changes fastest.
Arguments:
- start: float32 [256, 262144], P('grp', 'rows'), may hold values from -50 to 50
- momenta: float32 [256, 262144], P('grp', 'rows'), may hold values from -6 to 6
- observed: float32 [262144], P('rows'), may hold values from -6 to 6
- precision_obs: float32 [262144], P('rows'), may hold values from 0.5 to 4
- blocks: float32 [2048, 4, 128, 128], P('rows'), may hold values from -0.08 to 9
- block_cols: int32 [2048, 4], P('rows'), may hold values from 0 to 2047, as said below
- block_count: int32 [2048], P('rows'), may hold values from 2 to 4, as said below
- step_size: float32 [1], replicated, may hold values from 0.2 to 0.3
- trajectory: float32 [256], P('grp'), may hold values from 0.3 to 1.5
Outputs:
- position: float32 [256, 262144], P('grp', 'rows')
- momentum: float32 [256, 262144], P('grp', 'rows')
- chees: float32 [256], P('grp')
The draws below stay inside these ranges and needn't reach their ends.
Inputs may be any that keep to these rules, and one draw needn't show every extreme that they name: `block_cols`: slot 0 of block row r names r; slots 1 to 3 name distinct block rows r + k modulo 2048 with k from 1 to 64, and k = 64 occurs. `block_count`: 4 is reached.
All inputs are finite; a program needn't handle non-finite values.
Results may differ from the reference program's by a relative error of at most 0.0003.
Values sent between devices are 32-bit elements; how exact they have to be, the bound alone decides.
A program may use at most 192 MiB of HBM per device.

```python
import math
import jax
import jax.numpy as jnp
from jax import lax

BLOCK = 128
SLOTS = 4
BR_DEV = 64
CHAINS = 256
NBLOCKS = 2048
CELLS = 262144


def forced_row(key):
    return jax.random.randint(jax.random.fold_in(key, 11), (), 0, NBLOCKS).astype(jnp.int32)


def draw_block_cols(key, part):
    scores = jax.random.randint(jax.random.fold_in(key, 3), (NBLOCKS, BR_DEV), 0, 2 ** 20) * BR_DEV
    scores = scores + jnp.arange(BR_DEV, dtype=jnp.int32)[None, :]
    order = jnp.argsort(scores, axis=1).astype(jnp.int32)
    offsets = order[:, :SLOTS - 1] + 1
    special = jnp.concatenate([jnp.full((1,), BR_DEV, jnp.int32), jnp.arange(1, SLOTS - 1, dtype=jnp.int32)])
    row_ids = jnp.arange(NBLOCKS, dtype=jnp.int32)
    offsets = jnp.where(row_ids[:, None] == forced_row(key), special[None, :], offsets)
    upper_cols = jnp.mod(row_ids[:, None] + offsets, NBLOCKS)
    return jnp.concatenate([row_ids[:, None], upper_cols], axis=1).astype(jnp.int32)


def draw_block_count(key, part):
    counts = jax.random.randint(jax.random.fold_in(key, 5), (NBLOCKS,), 2, SLOTS + 1)
    row_ids = jnp.arange(NBLOCKS, dtype=jnp.int32)
    return jnp.where(row_ids == forced_row(key), SLOTS, counts).astype(jnp.int32)


def draw_blocks(key, part):
    raw_values = jax.random.uniform(jax.random.fold_in(key, 21), (NBLOCKS, SLOTS, BLOCK, BLOCK), jnp.float32, -1.0, 1.0)
    raw_values = 0.08 * raw_values
    symmetric = 0.5 * (raw_values + jnp.swapaxes(raw_values, 2, 3))
    diag_values = jax.random.uniform(jax.random.fold_in(key, 22), (NBLOCKS, SLOTS, BLOCK, BLOCK), jnp.float32, 5.0, 9.0)
    line_a = jnp.arange(BLOCK)[:, None]
    line_b = jnp.arange(BLOCK)[None, :]
    on_diag = (line_a == line_b)[None, None, :, :]
    slot_zero = jnp.where(on_diag, diag_values, symmetric)
    slot_ids = jnp.arange(SLOTS)[None, :, None, None]
    return jnp.where(slot_ids == 0, slot_zero, raw_values).astype(jnp.float32)


def draw_start(key, part):
    center = 1.5 * jax.random.truncated_normal(jax.random.fold_in(key, 31), -4.0, 4.0, (CELLS,), jnp.float32)
    ramp = jnp.exp(jnp.log(3.0) * jnp.arange(CELLS).astype(jnp.float32) / CELLS)
    jitter = jax.random.truncated_normal(jax.random.fold_in(key, 32), -4.0, 4.0, (CHAINS, CELLS), jnp.float32)
    chain_scale = jnp.ones((CHAINS, 1), jnp.float32)
    return (center[None, :] + 0.8 * chain_scale * ramp[None, :] * jitter).astype(jnp.float32)


def shard_levels(key, shape, pieces, least, largest):
    level, own = 1.0, jax.random.fold_in(key, 6)
    for dim, blocks in pieces:
        heights = jnp.exp(jax.random.uniform(jax.random.fold_in(own, dim), (blocks,), jnp.float32, least / len(pieces), largest / len(pieces)))
        level = level * jnp.repeat(heights, shape[dim] // blocks).reshape([-1 if axis == dim else 1 for axis in range(len(shape))])
    return level


def scatter_about(stream_key, dims, spread, limit, pieces=(), kind=jnp.bfloat16):
    result = jax.random.normal(stream_key, dims, jnp.float32) * spread
    if len(pieces) > 0:
        result = shard_levels(stream_key, dims, pieces, -0.22, 0.18) * result
    return jnp.clip(result, min=-limit, max=limit).astype(kind)


def setup_inputs(seed: int = 0) -> dict:
    key_of = jax.random.split(jax.random.key(seed), 10)
    start = draw_start(jax.random.fold_in(key_of[9], 71), 0)
    momenta = scatter_about(key_of[1], (CHAINS, CELLS), 1.0, 6.0, ((0, 4), (1, 32)), jnp.float32)
    observed = scatter_about(key_of[2], (CELLS,), 1.0, 6.0, ((0, 32),), jnp.float32)
    precision_obs = jnp.clip(jnp.exp(math.log(4.0) - 2.0794415 * jax.random.uniform(key_of[3], (CELLS,), jnp.float32) ** shard_levels(key_of[3], (CELLS,), ((0, 32),), -0.2, 0.2)), 0.5, 4.0)
    blocks = draw_blocks(jax.random.fold_in(key_of[9], 71), 0)
    block_cols = draw_block_cols(jax.random.fold_in(key_of[9], 71), 0)
    block_count = draw_block_count(jax.random.fold_in(key_of[9], 71), 0)
    step_size = jnp.clip(jax.random.uniform(key_of[7], (1,), jnp.float32, 0.2, 0.3), 0.2, 0.3)
    trajectory = jnp.clip(0.3 + 1.2 * jax.random.uniform(key_of[8], (CHAINS,), jnp.float32) ** shard_levels(key_of[8], (CHAINS,), ((0, 4),), -0.2, 0.2), 0.3, 1.5)
    return {"start": start, "momenta": momenta, "observed": observed, "precision_obs": precision_obs, "blocks": blocks, "block_cols": block_cols, "block_count": block_count, "step_size": step_size, "trajectory": trajectory}


PRECISE = lax.Precision.HIGHEST


def apply_precision(latent, blocks, block_cols, block_count):
    chain_total = latent.shape[0]
    block_side = blocks.shape[-1]
    nblocks = blocks.shape[0]
    slot_count = blocks.shape[1]
    block_tiles = latent.reshape(chain_total, nblocks, block_side)
    weights = (jnp.arange(slot_count, dtype=jnp.int32)[None, :] < block_count[:, None]).astype(jnp.float32)

    def group_step(spill_sum, group_id):
        first_row = (group_id * BR_DEV).astype(jnp.int32)
        band_blocks = lax.dynamic_slice_in_dim(blocks, first_row, BR_DEV, 0)
        group_cols = lax.dynamic_slice_in_dim(block_cols, first_row, BR_DEV, 0)
        group_weights = lax.dynamic_slice_in_dim(weights, first_row, BR_DEV, 0)
        group_tiles = lax.dynamic_slice_in_dim(block_tiles, first_row, BR_DEV, 1)
        picked = jnp.take(block_tiles, group_cols, axis=1)
        upper_rows = jnp.einsum("crsb,rsab,rs->cra", picked, band_blocks, group_weights, precision=PRECISE)
        transposed = jnp.einsum("cra,rsab,rs->crsb", group_tiles, band_blocks[:, 1:], group_weights[:, 1:], precision=PRECISE)
        spill_sum = spill_sum.at[:, group_cols[:, 1:]].add(transposed)
        return spill_sum, upper_rows

    spill_sum, upper_rows = lax.scan(group_step, jnp.zeros_like(block_tiles), jnp.arange(nblocks // BR_DEV, dtype=jnp.int32))
    upper_rows = jnp.transpose(upper_rows, (1, 0, 2, 3)).reshape(chain_total, nblocks, block_side)
    return (upper_rows + spill_sum).reshape(chain_total, -1)


def reference(start, momenta, observed, precision_obs, blocks, block_cols, block_count, step_size, trajectory):
    def gradient(latent):
        return -apply_precision(latent, blocks, block_cols, block_count) - precision_obs[None, :] * (latent - observed[None, :])

    step_len = step_size[0]
    half = momenta + (step_len / 2) * gradient(start)
    middle = start + step_len * half
    full = half + step_len * gradient(middle)
    position = middle + step_len * full
    momentum = full + (step_len / 2) * gradient(position)
    mean_start = jnp.sum(start, axis=0) / CHAINS
    mean_end = jnp.sum(position, axis=0) / CHAINS
    offset_start = start - mean_start[None, :]
    offset_end = position - mean_end[None, :]
    spread_start = jnp.sum(offset_start * offset_start, axis=1)
    spread_end = jnp.sum(offset_end * offset_end, axis=1)
    inner = jnp.sum(offset_end * momentum, axis=1)
    chees = trajectory * ((spread_end - spread_start) / CELLS) * (inner / CELLS)
    return position, momentum, chees
```

```python
import functools

import jax
import jax.numpy as jnp
from jax import lax
from jax.experimental import pallas as pl
from jax.experimental.pallas import tpu as pltpu
from jax.sharding import PartitionSpec as P

F32 = jnp.float32
BF16 = jnp.bfloat16
I32 = jnp.int32
NN = (((1,), (0,)), ((), ()))

SIDE = 128
SLOTS = 4
OFF = SLOTS - 1
BANDS = 64
CELLS = BANDS * SIDE
EDGES = BANDS * OFF
CHUNKS = 2
CH = 32
PIECES = 4
PB = BANDS // PIECES
PE = EDGES // PIECES
LOAD = 4
NLOAD = BANDS // LOAD
NSTAGE = 4


def dot(a, b):
    return lax.dot_general(a, b, NN, preferred_element_type=F32)


def split_rows(x):
    high = x.astype(BF16)
    low = (x - high.astype(F32)).astype(BF16)
    return jnp.concatenate([high, low], axis=0)


def split_lanes(x):
    high = x.astype(BF16)
    low = (x - high.astype(F32)).astype(BF16)
    return jnp.concatenate([high, low], axis=1)


def joined(p):
    return (p[:CH, :SIDE] + p[:CH, SIDE:]) + p[CH:, :SIDE]


def lanes(r):
    return pl.ds(pl.multiple_of(r * SIDE, SIDE), SIDE)


def edge_tables(cols_ref, count_ref, first, nblocks, table_ref):
    total = BANDS * SLOTS
    count = count_ref[...]
    sub = lax.broadcasted_iota(I32, (BANDS, BANDS), 0)
    lane = lax.broadcasted_iota(I32, (BANDS, BANDS), 1)
    row_id = lax.broadcasted_iota(I32, (1, BANDS), 1)
    col_id = lax.broadcasted_iota(I32, (BANDS, 1), 0)

    def column(row):
        return jnp.sum(jnp.where(sub == lane, row, 0), axis=1, keepdims=True)

    local, dest_col, key_row, key_col = [], [], [], []
    for s in range(1, SLOTS):
        d = cols_ref[s : s + 1, :] - first
        d = jnp.where(d < 0, d + nblocks, d)
        local.append(jnp.minimum(d, 2 * BANDS - 1))
        live = jnp.where(s < count, d, 0)
        key = live * total + row_id * OFF + (s - 1)
        dest_col.append(column(live))
        key_row.append(key)
        key_col.append(column(key))
    place = lax.broadcasted_iota(I32, (BANDS, total), 1)
    edge = jnp.zeros((1, total), I32)
    band = jnp.zeros((1, total), I32)
    dest = jnp.zeros((1, total), I32)
    before = jnp.zeros((1, total), I32)
    upto = jnp.zeros((1, total), I32)
    found = jnp.zeros((1, total), I32)

    def down(x):
        return jnp.sum(x, axis=0, keepdims=True)

    for s in range(OFF):
        rank = jnp.zeros((BANDS, 1), I32)
        for k in range(OFF):
            rank += jnp.sum(jnp.where(key_row[k] > key_col[s], 1, 0), axis=1, keepdims=True)
        here = rank == place
        edge += down(jnp.where(here, col_id * OFF + s, 0))
        band += down(jnp.where(here, col_id, 0))
        dest += down(jnp.where(here, dest_col[s], 0))
        before += down(jnp.where(rank + 1 == place, dest_col[s], 0))
        upto += down(jnp.where(dest_col[s] >= place, 1, 0))
        found += down(jnp.where(dest_col[s] == place, 1, 0))
    table_ref[0:1, :] = edge
    table_ref[1:2, :] = band
    table_ref[2:3, :] = jnp.where(dest == before, 1, 0)
    table_ref[3:4, :] = jnp.maximum(upto - 1, 0)
    table_ref[4:5, :] = jnp.minimum(found, 1)
    pad = jnp.zeros((1, total - BANDS), I32)
    for s in range(OFF):
        table_ref[5 + s : 6 + s, :] = jnp.concatenate([local[s], pad], axis=1)


def kernel(
    nrows,
    ngrp,
    chain_total,
    all_cells,
    start_hbm,
    momenta_hbm,
    observed_hbm,
    precision_hbm,
    blocks_hbm,
    cols_ref,
    count_ref,
    count_smem,
    step_smem,
    trajectory_ref,
    position_hbm,
    momentum_hbm,
    chees_ref,
    stage,
    flat,
    turned,
    v,
    m,
    split,
    u,
    sums,
    sent,
    next_v,
    carried,
    obs,
    prec,
    cell_sums,
    cell_all,
    mean,
    acc,
    part,
    part_y,
    table,
    smem,
    stage_sem,
    load_sem,
    out_sem,
    table_sem,
    up_send,
    up_recv,
    dn_send,
    dn_recv,
    x_send,
    x_recv,
    a_send,
    a_recv,
    b_send,
    b_recv,
):
    me = lax.axis_index("rows")
    grp = lax.axis_index("grp")
    up = lax.rem(me + nrows - 1, nrows)
    down = lax.rem(me + 1, nrows)
    near = 8
    far = nrows // near
    in_near = lax.rem(me, near)
    base = me - in_near
    in_far = me // near

    def near_peer(d):
        return base + lax.rem(in_near + d, near)

    def far_peer(d):
        return lax.rem(me + near * d, nrows)

    def load_v(c):
        return pltpu.make_async_copy(start_hbm.at[pl.ds(c * CH, CH)], v.at[c], load_sem.at[c])

    def load_m(c):
        return pltpu.make_async_copy(momenta_hbm.at[pl.ds(c * CH, CH)], m.at[c], load_sem.at[2 + c])

    load_obs = pltpu.make_async_copy(observed_hbm, obs, load_sem.at[4])
    load_prec = pltpu.make_async_copy(precision_hbm, prec, load_sem.at[5])

    def load_blocks(i):
        slot = lax.rem(i, NSTAGE)
        rows = pl.ds(i * LOAD * SLOTS, LOAD * SLOTS)
        return pltpu.make_async_copy(blocks_hbm.at[rows], stage.at[slot], stage_sem.at[slot])

    def store_position(c):
        return pltpu.make_async_copy(v.at[c], position_hbm.at[pl.ds(c * CH, CH)], out_sem.at[0, c])

    def store_momentum(c):
        return pltpu.make_async_copy(m.at[c], momentum_hbm.at[pl.ds(c * CH, CH)], out_sem.at[1, c])

    def send_up(g, c):
        par = lax.rem(g, 2)
        return pltpu.make_async_remote_copy(
            v.at[c], next_v.at[par, c], up_send.at[c], up_recv.at[par, c], device_id={"rows": up}
        )

    def send_down(g, c, p):
        par = lax.rem(g, 2)
        cells = pl.ds(pl.multiple_of(p * (PB * SIDE), PB * SIDE), PB * SIDE)
        return pltpu.make_async_remote_copy(
            sent.at[c, :, cells],
            carried.at[par, c, :, cells],
            dn_send.at[c, p],
            dn_recv.at[par, c, p],
            device_id={"rows": down},
        )

    def send_sums(which, d):
        return pltpu.make_async_remote_copy(
            cell_sums.at[which],
            cell_all.at[which, grp],
            x_send.at[which, d],
            x_recv.at[which, grp],
            device_id={"grp": lax.rem(grp + d, ngrp)},
        )

    def take_sums(which, d):
        slot = lax.rem(grp + d, ngrp)
        return pltpu.make_async_remote_copy(
            cell_sums.at[which],
            cell_all.at[which, slot],
            x_send.at[which, d],
            x_recv.at[which, slot],
            device_id={"grp": slot},
        )

    for c in range(CHUNKS):
        load_v(c).start()
    for i in range(NSTAGE):
        load_blocks(i).start()
    load_obs.start()
    load_prec.start()
    for c in range(CHUNKS):
        load_m(c).start()

    barrier = pltpu.get_barrier_semaphore()
    for peer in (up, down):
        pl.semaphore_signal(barrier, inc=1, device_id={"rows": peer})
    for d in range(1, ngrp):
        pl.semaphore_signal(barrier, inc=1, device_id={"grp": lax.rem(grp + d, ngrp)})
    for d in range(1, near):
        pl.semaphore_signal(barrier, inc=1, device_id={"rows": near_peer(d)})
    for d in range(1, far):
        pl.semaphore_signal(barrier, inc=1, device_id={"rows": far_peer(d)})

    edge_tables(cols_ref, count_ref, me * BANDS, nrows * BANDS, table)
    to_smem = pltpu.make_async_copy(table, smem, table_sem)
    to_smem.start()

    pl.semaphore_wait(barrier, 2 + (ngrp - 1) + (near - 1) + (far - 1))

    for c in range(CHUNKS):
        load_v(c).wait()
        send_up(0, c).start()

    def first_cells(r, _):
        total = jnp.zeros((1, SIDE), F32)
        for c in range(CHUNKS):
            x = v[c, :, lanes(r)]
            total += jnp.sum(x, axis=0, keepdims=True)
            split[c, r] = split_rows(x)
        cell_sums[0, pl.ds(r, 1), :] = total
        return 0

    lax.fori_loop(0, BANDS, first_cells, 0, unroll=4)
    for d in range(1, ngrp):
        send_sums(0, d).start()

    def take_blocks(i, _):
        load_blocks(i).wait()
        slot = lax.rem(i, NSTAGE)
        for k in range(LOAD):
            r = i * LOAD + k
            count = count_smem[r]
            for s in range(SLOTS):
                b = stage[slot, k * SLOTS + s]
                if s >= 2:
                    b = jnp.where(s < count, b, 0.0)
                pair = split_lanes(b)
                if s == 0:
                    turned[r, 0:SIDE, :] = pair
                else:
                    flat[r * OFF + (s - 1)] = pair

        @pl.when(i + NSTAGE < NLOAD)
        def _():
            load_blocks(i + NSTAGE).start()

        return 0

    lax.fori_loop(0, NLOAD, take_blocks, 0)
    to_smem.wait()

    def lower(g, c):
        def piece(q, total):
            p = PIECES - 1 - q

            def edge(k, total):
                place = q * PE + k
                term = joined(dot(split[c, smem[1, place]], flat[smem[0, place]]))
                total = jnp.where(smem[2, place] != 0, total, 0.0) + term
                sums[place] = total
                return total

            total = lax.fori_loop(0, PE, edge, total, unroll=16)

            def place_out(j, _):
                r = p * PB + j
                x = sums[smem[3, BANDS + r]]
                sent[c, :, lanes(r)] = jnp.where(smem[4, BANDS + r] != 0, x, 0.0)
                return 0

            lax.fori_loop(0, PB, place_out, 0, unroll=8)
            send_down(g, c, p).start()
            return total

        lax.fori_loop(0, PIECES, piece, jnp.zeros((CH, SIDE), F32))

        def place_own(r, _):
            x = sums[smem[3, r]]
            u[c, :, lanes(r)] = jnp.where(smem[4, r] != 0, x, 0.0)
            return 0

        lax.fori_loop(0, BANDS, place_own, 0, unroll=8)

    def first_lower(c, _):
        lower(0, c)
        return 0

    lax.fori_loop(0, CHUNKS, first_lower, 0)

    def turn(r, _):
        for s in range(OFF):
            x = flat[r * OFF + s]
            rows = pl.ds((s + 1) * SIDE, SIDE)
            turned[r, rows, :] = jnp.concatenate([x[:, :SIDE].T, x[:, SIDE:].T], axis=1)
        return 0

    lax.fori_loop(0, BANDS, turn, 0, unroll=2)

    def means(which):
        for d in range(1, ngrp):
            take_sums(which, d).wait_recv()
        cell_all[which, grp] = cell_sums[which]
        total = cell_all[which, 0]
        for k in range(1, ngrp):
            total = total + cell_all[which, k]
        mean[which] = total / chain_total

    def spread(which):
        for c in range(CHUNKS):

            def add(r, total):
                x = v[c, :, lanes(r)] - mean[which, pl.ds(r, 1), :]
                return total + x * x

            acc[which, c] = lax.fori_loop(0, BANDS, add, jnp.zeros((CH, SIDE), F32), unroll=8)

    means(0)
    spread(0)
    for c in range(CHUNKS):
        load_m(c).wait()
    load_obs.wait()
    load_prec.wait()

    step = step_smem[0]

    def upper(g, c):
        par = lax.rem(g, 2)
        send_up(g, c).wait_recv()

        def take(r, _):
            split[c, BANDS + r] = split_rows(next_v[par, c, :, lanes(r)])
            return 0

        lax.fori_loop(0, BANDS, take, 0, unroll=8)

        def row(r, _):
            rows = [split[c, r]] + [split[c, smem[5 + s, r]] for s in range(OFF)]
            term = joined(dot(jnp.concatenate(rows, axis=1), turned[r]))
            u[c, :, lanes(r)] = u[c, :, lanes(r)] + term
            return 0

        lax.fori_loop(0, BANDS, row, 0, unroll=8)

    def gradient(g, c, r):
        par = lax.rem(g, 2)
        x = v[c, :, lanes(r)]
        pull = prec[pl.ds(r, 1), :] * (x - obs[pl.ds(r, 1), :])
        return x, -(u[c, :, lanes(r)] + carried[par, c, :, lanes(r)]) - pull

    def move(g, c):
        kick = jnp.where(g == 0, step / 2, step)
        send_up(g, c).wait_send()

        def piece(q, _):
            p = PIECES - 1 - q
            send_down(g, c, p).wait_recv()

            def band(j, _):
                r = p * PB + j
                x, grad = gradient(g, c, r)
                mom = m[c, :, lanes(r)] + kick * grad
                m[c, :, lanes(r)] = mom
                x = x + step * mom
                v[c, :, lanes(r)] = x
                split[c, r] = split_rows(x)
                here = jnp.sum(x, axis=0, keepdims=True)
                old = jnp.where(c == 0, 0.0, cell_sums[1, pl.ds(r, 1), :])
                cell_sums[1, pl.ds(r, 1), :] = old + here
                return 0

            return lax.fori_loop(0, PB, band, 0, unroll=4)

        lax.fori_loop(0, PIECES, piece, 0)

    def finish(g, c):
        send_up(g, c).wait_send()

        def piece(q, total):
            p = PIECES - 1 - q
            send_down(g, c, p).wait_recv()

            def band(j, total):
                r = p * PB + j
                x, grad = gradient(g, c, r)
                mom = m[c, :, lanes(r)] + (step / 2) * grad
                m[c, :, lanes(r)] = mom
                return total + (x - mean[1, pl.ds(r, 1), :]) * mom

            return lax.fori_loop(0, PB, band, total, unroll=4)

        acc[2, c] = lax.fori_loop(0, PIECES, piece, jnp.zeros((CH, SIDE), F32))

    def stage_of(t, _):
        g = t // CHUNKS
        c = lax.rem(t, CHUNKS)
        upper(g, c)

        @pl.when(g < 2)
        def _():
            move(g, c)
            send_up(g + 1, c).start()

            @pl.when(g == 1)
            def _():
                store_position(c).start()

            for p in range(PIECES):
                send_down(g, c, p).wait_send()
            lower(g + 1, c)

        @pl.when(t == 3)
        def _():
            for d in range(1, ngrp):
                send_sums(1, d).start()

        @pl.when(t == 4)
        def _():
            means(1)

        @pl.when(g == 2)
        def _():
            finish(g, c)
            store_momentum(c).start()

        @pl.when(t == 4)
        def _():
            spread(1)

        return 0

    lax.fori_loop(0, 3 * CHUNKS, stage_of, 0)

    sub = lax.broadcasted_iota(I32, (CH, SIDE), 0)
    lane = lax.broadcasted_iota(I32, (CH, SIDE), 1)
    inner = jnp.zeros((1, SIDE), F32)
    change = jnp.zeros((1, SIDE), F32)
    for c in range(CHUNKS):
        here = lane == sub + c * CH
        column = jnp.sum(acc[2, c], axis=1, keepdims=True)
        inner += jnp.sum(jnp.where(here, column, 0.0), axis=0, keepdims=True)
        column = jnp.sum(acc[1, c], axis=1, keepdims=True) - jnp.sum(acc[0, c], axis=1, keepdims=True)
        change += jnp.sum(jnp.where(here, column, 0.0), axis=0, keepdims=True)
    own = jnp.concatenate([inner, change, jnp.zeros((6, SIDE), F32)], axis=0)

    def near_copy(slot, d):
        return pltpu.make_async_remote_copy(
            part.at[in_near], part.at[slot], a_send.at[d], a_recv.at[slot], device_id={"rows": near_peer(d)}
        )

    def far_copy(slot, d):
        return pltpu.make_async_remote_copy(
            part_y.at[in_far], part_y.at[slot], b_send.at[d], b_recv.at[slot], device_id={"rows": far_peer(d)}
        )

    part[in_near] = own
    for d in range(1, near):
        near_copy(in_near, d).start()
    for d in range(1, near):
        near_copy(lax.rem(in_near + d, near), d).wait_recv()
    total = part[0]
    for k in range(1, near):
        total = total + part[k]
    part_y[in_far] = total
    for d in range(1, far):
        far_copy(in_far, d).start()
    for d in range(1, far):
        far_copy(lax.rem(in_far + d, far), d).wait_recv()
    total = part_y[0]
    for k in range(1, far):
        total = total + part_y[k]
    chees_ref[...] = (
        trajectory_ref[...] * (total[1:2, : CHUNKS * CH] / all_cells) * (total[0:1, : CHUNKS * CH] / all_cells)
    )

    for d in range(1, near):
        near_copy(in_near, d).wait_send()
    for d in range(1, far):
        far_copy(in_far, d).wait_send()
    for which in range(2):
        for d in range(1, ngrp):
            send_sums(which, d).wait_send()
    for c in range(CHUNKS):
        for p in range(PIECES):
            send_down(2, c, p).wait_send()
        store_position(c).wait()
        store_momentum(c).wait()


def on_device(start, momenta, observed, precision_obs, blocks, block_cols, block_count, step_size, trajectory):
    nrows = lax.axis_size("rows")
    ngrp = lax.axis_size("grp")
    far = nrows // 8
    hbm = pl.BlockSpec(memory_space=pl.ANY)
    vmem = pl.BlockSpec(memory_space=pltpu.VMEM)
    smem = pl.BlockSpec(memory_space=pltpu.SMEM)
    dma = pltpu.SemaphoreType.DMA
    chains = CHUNKS * CH
    position, momentum, chees = pl.pallas_call(
        functools.partial(kernel, nrows, ngrp, chains * ngrp, CELLS * nrows),
        out_shape=(
            jax.ShapeDtypeStruct((chains, CELLS), F32),
            jax.ShapeDtypeStruct((chains, CELLS), F32),
            jax.ShapeDtypeStruct((1, chains), F32),
        ),
        in_specs=[hbm, hbm, hbm, hbm, hbm, vmem, vmem, smem, smem, vmem],
        out_specs=(hbm, hbm, vmem),
        scratch_shapes=[
            pltpu.VMEM((NSTAGE, LOAD * SLOTS, SIDE, SIDE), F32),
            pltpu.VMEM((EDGES, SIDE, 2 * SIDE), BF16),
            pltpu.VMEM((BANDS, SLOTS * SIDE, 2 * SIDE), BF16),
            pltpu.VMEM((CHUNKS, CH, CELLS), F32),
            pltpu.VMEM((CHUNKS, CH, CELLS), F32),
            pltpu.VMEM((CHUNKS, 2 * BANDS, 2 * CH, SIDE), BF16),
            pltpu.VMEM((CHUNKS, CH, CELLS), F32),
            pltpu.VMEM((EDGES, CH, SIDE), F32),
            pltpu.VMEM((CHUNKS, CH, CELLS), F32),
            pltpu.VMEM((2, CHUNKS, CH, CELLS), F32),
            pltpu.VMEM((2, CHUNKS, CH, CELLS), F32),
            pltpu.VMEM((BANDS, SIDE), F32),
            pltpu.VMEM((BANDS, SIDE), F32),
            pltpu.VMEM((2, BANDS, SIDE), F32),
            pltpu.VMEM((2, ngrp, BANDS, SIDE), F32),
            pltpu.VMEM((2, BANDS, SIDE), F32),
            pltpu.VMEM((3, CHUNKS, CH, SIDE), F32),
            pltpu.VMEM((8, 8, SIDE), F32),
            pltpu.VMEM((far, 8, SIDE), F32),
            pltpu.VMEM((8, SLOTS * BANDS), I32),
            pltpu.SMEM((8, SLOTS * BANDS), I32),
            dma((NSTAGE,)),
            dma((6,)),
            dma((2, CHUNKS)),
            dma,
            dma((CHUNKS,)),
            dma((2, CHUNKS)),
            dma((CHUNKS, PIECES)),
            dma((2, CHUNKS, PIECES)),
            dma((2, ngrp)),
            dma((2, ngrp)),
            dma((8,)),
            dma((8,)),
            dma((far,)),
            dma((far,)),
        ],
        compiler_params=pltpu.CompilerParams(
            collective_id=0, has_side_effects=True, vmem_limit_bytes=60 * 1024 * 1024
        ),
    )(
        start,
        momenta,
        observed.reshape(BANDS, SIDE),
        precision_obs.reshape(BANDS, SIDE),
        blocks.reshape(BANDS * SLOTS, SIDE, SIDE),
        block_cols.T,
        block_count.reshape(1, BANDS),
        block_count,
        step_size,
        trajectory.reshape(1, chains),
    )
    return position, momentum, chees.reshape(chains)


def solution(mesh):
    placed = (
        P("grp", "rows"),
        P("grp", "rows"),
        P("rows"),
        P("rows"),
        P("rows", None, None, None),
        P("rows", None),
        P("rows"),
        P(),
        P("grp"),
    )
    return jax.shard_map(
        on_device,
        mesh=mesh,
        in_specs=placed,
        out_specs=(P("grp", "rows"), P("grp", "rows"), P("grp")),
        check_vma=False,
    )
```

```python
import functools

import jax
import jax.numpy as jnp
from jax import lax
from jax.experimental import pallas as pl
from jax.experimental.pallas import tpu as pltpu
from jax.sharding import PartitionSpec as P

F32 = jnp.float32
BF16 = jnp.bfloat16
I32 = jnp.int32
NN = (((1,), (0,)), ((), ()))

SIDE = 128
SLOTS = 4
OFF = SLOTS - 1
BANDS = 64
CELLS = BANDS * SIDE
EDGES = BANDS * OFF
CHUNKS = 2
CH = 32
PIECES = 4
PB = BANDS // PIECES
PE = EDGES // PIECES
LOAD = 4
NLOAD = BANDS // LOAD
NSTAGE = 4
STRIPS = 4


def dot(a, b):
    return lax.dot_general(a, b, NN, preferred_element_type=F32)


def split_rows(x):
    high = x.astype(BF16)
    low = (x - high.astype(F32)).astype(BF16)
    return jnp.concatenate([high, low], axis=0)


def split_lanes(x):
    high = x.astype(BF16)
    low = (x - high.astype(F32)).astype(BF16)
    return jnp.concatenate([high, low], axis=1)


def joined(p):
    return (p[:CH, :SIDE] + p[:CH, SIDE:]) + p[CH:, :SIDE]


def joined_both(p):
    return jnp.concatenate([joined(p[c * 2 * CH : (c + 1) * 2 * CH]) for c in range(CHUNKS)], axis=0)


def lanes(r):
    return pl.ds(pl.multiple_of(r * SIDE, SIDE), SIDE)


def edge_tables(cols_ref, count_ref, first, nblocks, table_ref):
    total = BANDS * SLOTS
    count = count_ref[...]
    sub = lax.broadcasted_iota(I32, (BANDS, BANDS), 0)
    lane = lax.broadcasted_iota(I32, (BANDS, BANDS), 1)
    row_id = lax.broadcasted_iota(I32, (1, BANDS), 1)
    col_id = lax.broadcasted_iota(I32, (BANDS, 1), 0)

    def column(row):
        return jnp.sum(jnp.where(sub == lane, row, 0), axis=1, keepdims=True)

    local, dest_col, key_row, key_col = [], [], [], []
    for s in range(1, SLOTS):
        d = cols_ref[s : s + 1, :] - first
        d = jnp.where(d < 0, d + nblocks, d)
        local.append(jnp.minimum(d, 2 * BANDS - 1))
        live = jnp.where(s < count, d, 0)
        key = (row_id // PB) * (1 << 20) + live * total + row_id * OFF + (s - 1)
        dest_col.append(column(live))
        key_row.append(key)
        key_col.append(column(key))
    place = lax.broadcasted_iota(I32, (BANDS, total), 1)
    edge = jnp.zeros((1, total), I32)
    band = jnp.zeros((1, total), I32)
    dest = jnp.zeros((1, total), I32)
    before = jnp.zeros((1, total), I32)

    def down(x):
        return jnp.sum(x, axis=0, keepdims=True)

    for s in range(OFF):
        rank = jnp.zeros((BANDS, 1), I32)
        for k in range(OFF):
            rank += jnp.sum(jnp.where(key_row[k] > key_col[s], 1, 0), axis=1, keepdims=True)
        here = rank == place
        edge += down(jnp.where(here, col_id * OFF + s, 0))
        band += down(jnp.where(here, col_id, 0))
        dest += down(jnp.where(here, dest_col[s], 0))
        before += down(jnp.where(rank + 1 == place, dest_col[s], 0))
    table_ref[0:1, :] = edge
    table_ref[1:2, :] = band
    table_ref[2:3, :] = jnp.where(dest == before, 1, 0)
    pad = jnp.zeros((1, total - BANDS), I32)
    for s in range(OFF):
        table_ref[3 + s : 4 + s, :] = jnp.concatenate([local[s], pad], axis=1)
    spot = lax.broadcasted_iota(I32, (PB, total), 1)
    spot = jnp.where(spot < SIDE, spot, spot - SIDE)
    side = lax.broadcasted_iota(I32, (1, total), 1)
    for q in range(PIECES):
        upto = jnp.zeros((1, total), I32)
        found = jnp.zeros((1, total), I32)
        for s in range(OFF):
            d = dest_col[s][q * PB : (q + 1) * PB, :]
            upto += down(jnp.where(d >= spot, 1, 0))
            found += down(jnp.where(d == spot, 1, 0))
        last = jnp.maximum(upto - 1, 0)
        table_ref[6 + q : 7 + q, :] = jnp.where(side < SIDE, last, jnp.minimum(found, 1))


def kernel(
    nrows,
    ngrp,
    chain_total,
    all_cells,
    start_hbm,
    momenta_hbm,
    observed_hbm,
    precision_hbm,
    blocks_hbm,
    cols_ref,
    count_ref,
    count_smem,
    step_smem,
    trajectory_ref,
    position_hbm,
    momentum_hbm,
    chees_ref,
    stage,
    flat,
    turned,
    v,
    m,
    split,
    u,
    sums,
    next_v,
    carried,
    obs,
    prec,
    cell_sums,
    cell_all,
    mean,
    mean_next,
    acc,
    part,
    part_y,
    table,
    smem,
    stage_sem,
    load_sem,
    out_sem,
    momentum_sem,
    table_sem,
    up_send,
    up_recv,
    dn_send,
    dn_recv,
    x_send,
    x_recv,
    a_send,
    a_recv,
    b_send,
    b_recv,
    mean_send,
    mean_recv,
):
    me = lax.axis_index("rows")
    grp = lax.axis_index("grp")
    up = lax.rem(me + nrows - 1, nrows)
    down = lax.rem(me + 1, nrows)
    near = 8
    far = nrows // near
    in_near = lax.rem(me, near)
    base = me - in_near
    in_far = me // near

    def near_peer(d):
        return base + lax.rem(in_near + d, near)

    def far_peer(d):
        return lax.rem(me + near * d, nrows)

    def piece_cells(p):
        return pl.ds(pl.multiple_of(p * (PB * SIDE), PB * SIDE), PB * SIDE)

    def load_v(c):
        return pltpu.make_async_copy(start_hbm.at[pl.ds(c * CH, CH)], v.at[c], load_sem.at[c])

    def load_m(c):
        return pltpu.make_async_copy(momenta_hbm.at[pl.ds(c * CH, CH)], m.at[c], load_sem.at[2 + c])

    load_obs = pltpu.make_async_copy(observed_hbm, obs, load_sem.at[4])
    load_prec = pltpu.make_async_copy(precision_hbm, prec, load_sem.at[5])

    def load_band(i):
        per = PB // LOAD
        return ((PIECES - 1 - i // per) * per + lax.rem(i, per)) * LOAD

    def load_blocks(i):
        slot = lax.rem(i, NSTAGE)
        rows = pl.ds(load_band(i) * SLOTS, LOAD * SLOTS)
        return pltpu.make_async_copy(blocks_hbm.at[rows], stage.at[slot], stage_sem.at[slot])

    def store_position(c):
        return pltpu.make_async_copy(v.at[c], position_hbm.at[pl.ds(c * CH, CH)], out_sem.at[c])

    def store_momentum(c, p):
        cells = piece_cells(p)
        return pltpu.make_async_copy(
            m.at[c, :, cells], momentum_hbm.at[pl.ds(c * CH, CH), cells], momentum_sem.at[c, p]
        )

    def send_up(g, c, p):
        par = lax.rem(g, 2)
        return pltpu.make_async_remote_copy(
            v.at[c, :, piece_cells(p)],
            next_v.at[par, c, :, piece_cells(p)],
            up_send.at[c, p],
            up_recv.at[par, c, p],
            device_id={"rows": up},
        )

    def send_down(g, c, p):
        par = lax.rem(g, 2)
        return pltpu.make_async_remote_copy(
            u.at[c, :, pl.ds(pl.multiple_of(CELLS + p * (PB * SIDE), PB * SIDE), PB * SIDE)],
            carried.at[par, c, :, piece_cells(p)],
            dn_send.at[c, p],
            dn_recv.at[par, c, p],
            device_id={"rows": down},
        )

    def send_sums(which, d):
        return pltpu.make_async_remote_copy(
            cell_sums.at[which],
            cell_all.at[which, grp],
            x_send.at[which, d],
            x_recv.at[which, grp],
            device_id={"grp": lax.rem(grp + d, ngrp)},
        )

    def take_sums(which, d):
        slot = lax.rem(grp + d, ngrp)
        return pltpu.make_async_remote_copy(
            cell_sums.at[which],
            cell_all.at[which, slot],
            x_send.at[which, d],
            x_recv.at[which, slot],
            device_id={"grp": slot},
        )

    send_mean = pltpu.make_async_remote_copy(
        mean.at[1], mean_next, mean_send, mean_recv, device_id={"rows": up}
    )

    for c in range(CHUNKS):
        load_v(c).start()
    for i in range(NSTAGE):
        load_blocks(i).start()
    load_obs.start()
    load_prec.start()

    barrier = pltpu.get_barrier_semaphore()
    for peer in (up, down):
        pl.semaphore_signal(barrier, inc=1, device_id={"rows": peer})
    for d in range(1, ngrp):
        pl.semaphore_signal(barrier, inc=1, device_id={"grp": lax.rem(grp + d, ngrp)})
    for d in range(1, near):
        pl.semaphore_signal(barrier, inc=1, device_id={"rows": near_peer(d)})
    for d in range(1, far):
        pl.semaphore_signal(barrier, inc=1, device_id={"rows": far_peer(d)})

    pl.semaphore_wait(barrier, 2 + (ngrp - 1) + (near - 1) + (far - 1))

    for c in range(CHUNKS):
        load_v(c).wait()
        for p in range(PIECES):
            send_up(0, c, p).start()

    edge_tables(cols_ref, count_ref, me * BANDS, nrows * BANDS, table)
    to_smem = pltpu.make_async_copy(table, smem, table_sem)
    to_smem.start()

    def first_cells(r, _):
        total = jnp.zeros((1, SIDE), F32)
        for c in range(CHUNKS):
            x = v[c, :, lanes(r)]
            total += jnp.sum(x, axis=0, keepdims=True)
            split[c, r] = split_rows(x)
        cell_sums[0, pl.ds(r, 1), :] = total
        return 0

    lax.fori_loop(0, BANDS, first_cells, 0, unroll=4)
    for d in range(1, ngrp):
        send_sums(0, d).start()

    def take_blocks(i, _):
        load_blocks(i).wait()
        slot = lax.rem(i, NSTAGE)
        for k in range(LOAD):
            r = load_band(i) + k
            count = count_smem[r]
            for s in range(SLOTS):
                b = stage[slot, k * SLOTS + s]
                if s >= 2:
                    b = jnp.where(s < count, b, 0.0)
                pair = split_lanes(b)
                if s == 0:
                    turned[r, 0:SIDE, :] = pair
                else:
                    flat[r * OFF + (s - 1)] = pair

        @pl.when(i + NSTAGE < NLOAD)
        def _():
            load_blocks(i + NSTAGE).start()

        return 0

    to_smem.wait()

    def spread_out(chunks, p):
        def found(r, i):
            x = sums[smem[6 + p, r], i * CH : (i + 1) * CH, :]
            return jnp.where(smem[6 + p, SIDE + r] != 0, x, 0.0)

        def fresh(j, _):
            r = p * PB + j
            for i, c in enumerate(chunks):
                u[c, :, lanes(r)] = found(r, i)
            return 0

        def more(j, _):
            r = p * PB + j
            for i, c in enumerate(chunks):
                u[c, :, lanes(r)] = u[c, :, lanes(r)] + found(r, i)
            return 0

        lax.fori_loop(0, PB, fresh, 0, unroll=8)

        @pl.when(p == PIECES - 1)
        def _():
            lax.fori_loop(PB, PB + BANDS, fresh, 0, unroll=8)

        @pl.when(p < PIECES - 1)
        def _():
            lax.fori_loop(PB, PB + BANDS, more, 0, unroll=8)

    def quarter(g, c, p):
        def edge(k, total):
            place = (PIECES - 1 - p) * PE + k
            term = joined(dot(split[c, smem[1, place]], flat[smem[0, place]]))
            total = jnp.where(smem[2, place] != 0, total, 0.0) + term
            sums[k, :CH, :] = total
            return total

        place = (PIECES - 1 - p) * PE
        total = joined(dot(split[c, smem[1, place]], flat[smem[0, place]]))
        sums[0, :CH, :] = total
        lax.fori_loop(1, PE, edge, total, unroll=PE - 1)
        spread_out((c,), p)
        send_down(g, c, p).start()

    def first_quarter(q, _):
        p = PIECES - 1 - q
        per = NLOAD // PIECES
        lax.fori_loop(q * per, (q + 1) * per, take_blocks, 0)

        def edges(i, total):
            r = p * PB + i
            for s in range(OFF):
                place = q * PE + i * OFF + s
                band = smem[1, place]
                both = jnp.concatenate([split[c, band] for c in range(CHUNKS)], axis=0)
                term = joined_both(dot(both, flat[smem[0, place]]))
                keep = smem[2, place]
                if s == 0:
                    keep = jnp.where(i == 0, 0, keep)
                total = jnp.where(keep != 0, total, 0.0) + term
                sums[i * OFF + s] = total
                x = flat[r * OFF + s]
                turned[r, (s + 1) * SIDE : (s + 2) * SIDE, :] = jnp.concatenate(
                    [x[:, :SIDE].T, x[:, SIDE:].T], axis=1
                )
            return total

        lax.fori_loop(0, PB, edges, jnp.zeros((CHUNKS * CH, SIDE), F32), unroll=8)
        spread_out(range(CHUNKS), p)
        send_down(0, 0, p).start()
        return 0

    lax.fori_loop(0, PIECES, first_quarter, 0)
    for c in range(CHUNKS):
        load_m(c).start()
    for p in reversed(range(PIECES)):
        send_down(0, 1, p).start()

    def means(which):
        for d in range(1, ngrp):
            take_sums(which, d).wait_recv()
        cell_all[which, grp] = cell_sums[which]
        total = cell_all[which, 0]
        for k in range(1, ngrp):
            total = total + cell_all[which, k]
        mean[which] = total / chain_total

    def spread(which):
        for c in range(CHUNKS):

            def add(r, total):
                x = v[c, :, lanes(r)] - mean[which, pl.ds(r, 1), :]
                return total + x * x

            acc[which, c] = lax.fori_loop(0, BANDS, add, jnp.zeros((CH, SIDE), F32), unroll=8)

    means(0)
    spread(0)
    for c in range(CHUNKS):
        load_m(c).wait()
    load_obs.wait()
    load_prec.wait()

    step = step_smem[0]

    def upper(g, c):
        par = lax.rem(g, 2)

        def piece(p, _):
            send_up(g, c, p).wait_recv()

            def take(j, _):
                r = p * PB + j
                split[c, BANDS + r] = split_rows(next_v[par, c, :, lanes(r)])
                return 0

            lax.fori_loop(0, PB, take, 0, unroll=8)

            def row(j, _):
                r = p * PB + j
                rows = [split[c, r]] + [split[c, smem[3 + s, r]] for s in range(OFF)]
                term = joined(dot(jnp.concatenate(rows, axis=1), turned[r]))
                u[c, :, lanes(r)] = u[c, :, lanes(r)] + term
                return 0

            return lax.fori_loop(0, PB, row, 0, unroll=PB)

        lax.fori_loop(0, PIECES, piece, 0)

    def gradient(g, c, r):
        par = lax.rem(g, 2)
        x = v[c, :, lanes(r)]
        pull = prec[pl.ds(r, 1), :] * (x - obs[pl.ds(r, 1), :])
        return x, -(u[c, :, lanes(r)] + carried[par, c, :, lanes(r)]) - pull

    def move(g, c):
        kick = jnp.where(g == 0, step / 2, step)
        for p in range(PIECES):
            send_up(g, c, p).wait_send()

        def piece(q, _):
            p = PIECES - 1 - q
            send_down(g, c, p).wait_recv()

            def band(j, _):
                r = p * PB + j
                x, grad = gradient(g, c, r)
                mom = m[c, :, lanes(r)] + kick * grad
                m[c, :, lanes(r)] = mom
                x = x + step * mom
                v[c, :, lanes(r)] = x
                split[c, r] = split_rows(x)
                here = jnp.sum(x, axis=0, keepdims=True)
                old = jnp.where(c == 0, 0.0, cell_sums[1, pl.ds(r, 1), :])
                cell_sums[1, pl.ds(r, 1), :] = old + here
                return 0

            return lax.fori_loop(0, PB, band, 0, unroll=4)

        lax.fori_loop(0, PIECES, piece, 0)

    def finish(g, c):
        for p in range(PIECES):
            send_up(g, c, p).wait_send()

        def piece(q, _):
            p = PIECES - 1 - q
            send_down(g, c, p).wait_recv()

            def band(j, _):
                r = p * PB + j
                x, grad = gradient(g, c, r)
                m[c, :, lanes(r)] = m[c, :, lanes(r)] + (step / 2) * grad
                return 0

            lax.fori_loop(0, PB, band, 0, unroll=4)
            store_momentum(c, p).start()
            return 0

        lax.fori_loop(0, PIECES, piece, 0)

    def inner_early(c):
        def band(r, total):
            x = v[c, :, lanes(r)]
            pull = prec[pl.ds(r, 1), :] * (x - obs[pl.ds(r, 1), :])
            mom = m[c, :, lanes(r)] - (step / 2) * (u[c, :, lanes(r)] + pull)
            ahead = next_v[0, c, :, lanes(r)] - mean_next[pl.ds(r, 1), :]
            total = total + (x - mean[1, pl.ds(r, 1), :]) * mom
            return total - (step / 2) * (ahead * u[c, :, lanes(BANDS + r)])

        acc[2, c] = lax.fori_loop(0, BANDS, band, jnp.zeros((CH, SIDE), F32), unroll=4)

    def inner_late(c):
        def band(r, total):
            return total + (v[c, :, lanes(r)] - mean[1, pl.ds(r, 1), :]) * m[c, :, lanes(r)]

        acc[2, c] = lax.fori_loop(0, BANDS, band, jnp.zeros((CH, SIDE), F32), unroll=8)

    def near_copy(slot, d):
        return pltpu.make_async_remote_copy(
            part.at[in_near], part.at[slot], a_send.at[d], a_recv.at[slot], device_id={"rows": near_peer(d)}
        )

    def far_copy(slot, d):
        return pltpu.make_async_remote_copy(
            part_y.at[in_far], part_y.at[slot], b_send.at[d], b_recv.at[slot], device_id={"rows": far_peer(d)}
        )

    def start_sum():
        sub = lax.broadcasted_iota(I32, (CH, SIDE), 0)
        lane = lax.broadcasted_iota(I32, (CH, SIDE), 1)
        inner = jnp.zeros((1, SIDE), F32)
        change = jnp.zeros((1, SIDE), F32)
        for c in range(CHUNKS):
            here = lane == sub + c * CH
            column = jnp.sum(acc[2, c], axis=1, keepdims=True)
            inner += jnp.sum(jnp.where(here, column, 0.0), axis=0, keepdims=True)
            column = jnp.sum(acc[1, c], axis=1, keepdims=True) - jnp.sum(acc[0, c], axis=1, keepdims=True)
            change += jnp.sum(jnp.where(here, column, 0.0), axis=0, keepdims=True)
        own = jnp.concatenate([inner, change, jnp.zeros((6, SIDE), F32)], axis=0)

        part_y[in_far] = own
        for d in range(1, far):
            far_copy(in_far, d).start()
        for d in range(1, far):
            far_copy(lax.rem(in_far + d, far), d).wait_recv()
        total = part_y[0]
        for k in range(1, far):
            total = total + part_y[k]
        part[in_near] = total
        for d in range(1, near):
            near_copy(in_near, d).start()

    def end_sum():
        for d in range(1, near):
            near_copy(lax.rem(in_near + d, near), d).wait_recv()
        total = part[0]
        for k in range(1, near):
            total = total + part[k]
        chees_ref[...] = (
            trajectory_ref[...] * (total[1:2, : CHUNKS * CH] / all_cells) * (total[0:1, : CHUNKS * CH] / all_cells)
        )
        for d in range(1, near):
            near_copy(in_near, d).wait_send()
        for d in range(1, far):
            far_copy(in_far, d).wait_send()

    def stage_of(t, _):
        g = t // CHUNKS
        c = lax.rem(t, CHUNKS)
        upper(g, c)

        @pl.when(g < 2)
        def _():
            move(g, c)
            for p in range(PIECES):
                send_up(g + 1, c, p).start()

            @pl.when(g == 1)
            def _():
                store_position(c).start()

            @pl.when(t == 3)
            def _():
                for d in range(1, ngrp):
                    send_sums(1, d).start()

            for p in range(PIECES):
                send_down(g, c, p).wait_send()

            def again(q, _):
                quarter(g + 1, c, PIECES - 1 - q)
                return 0

            lax.fori_loop(0, PIECES, again, 0)

        @pl.when(t == 4)
        def _():
            means(1)
            send_mean.start()

        @pl.when(t == 5)
        def _():
            send_mean.wait_recv()
            inner_early(1)
            start_sum()

        @pl.when(g == 2)
        def _():
            finish(g, c)

        @pl.when(t == 4)
        def _():
            inner_late(0)
            spread(1)

        return 0

    lax.fori_loop(0, 3 * CHUNKS, stage_of, 0)
    end_sum()

    send_mean.wait_send()
    for which in range(2):
        for d in range(1, ngrp):
            send_sums(which, d).wait_send()
    for c in range(CHUNKS):
        for p in range(PIECES):
            send_down(2, c, p).wait_send()
        store_position(c).wait()
        for p in range(PIECES):
            store_momentum(c, p).wait()


def hand_over(position_ref, momentum_ref, chees_ref, position_out, momentum_out, chees_out, held, in_sem, out_sem):
    part = CHUNKS * CH // STRIPS
    reads, writes = [], []
    for k, (a, b) in enumerate(((position_ref, position_out), (momentum_ref, momentum_out))):
        for i in range(STRIPS):
            rows = pl.ds(i * part, part)
            reads.append(pltpu.make_async_copy(a.at[rows], held.at[k, rows], in_sem.at[k, i]))
            writes.append(pltpu.make_async_copy(held.at[k, rows], b.at[rows], out_sem.at[k, i]))
    for copy in reads:
        copy.start()
    chees_out[...] = chees_ref[...]
    for read, write in zip(reads, writes):
        read.wait()
        write.start()
    for copy in writes:
        copy.wait()


def on_device(start, momenta, observed, precision_obs, blocks, block_cols, block_count, step_size, trajectory):
    nrows = lax.axis_size("rows")
    ngrp = lax.axis_size("grp")
    far = nrows // 8
    hbm = pl.BlockSpec(memory_space=pltpu.HBM)
    vmem = pl.BlockSpec(memory_space=pltpu.VMEM)
    smem = pl.BlockSpec(memory_space=pltpu.SMEM)
    dma = pltpu.SemaphoreType.DMA
    chains = CHUNKS * CH
    position, momentum, chees = pl.pallas_call(
        functools.partial(kernel, nrows, ngrp, chains * ngrp, CELLS * nrows),
        out_shape=(
            jax.ShapeDtypeStruct((chains, CELLS), F32),
            jax.ShapeDtypeStruct((chains, CELLS), F32),
            jax.ShapeDtypeStruct((1, chains), F32),
        ),
        in_specs=[hbm, hbm, hbm, hbm, hbm, vmem, vmem, smem, smem, vmem],
        out_specs=(hbm, hbm, vmem),
        scratch_shapes=[
            pltpu.VMEM((NSTAGE, LOAD * SLOTS, SIDE, SIDE), F32),
            pltpu.VMEM((EDGES, SIDE, 2 * SIDE), BF16),
            pltpu.VMEM((BANDS, SLOTS * SIDE, 2 * SIDE), BF16),
            pltpu.VMEM((CHUNKS, CH, CELLS), F32),
            pltpu.VMEM((CHUNKS, CH, CELLS), F32),
            pltpu.VMEM((CHUNKS, 2 * BANDS, 2 * CH, SIDE), BF16),
            pltpu.VMEM((CHUNKS, CH, 2 * CELLS), F32),
            pltpu.VMEM((PE, CHUNKS * CH, SIDE), F32),
            pltpu.VMEM((2, CHUNKS, CH, CELLS), F32),
            pltpu.VMEM((2, CHUNKS, CH, CELLS), F32),
            pltpu.VMEM((BANDS, SIDE), F32),
            pltpu.VMEM((BANDS, SIDE), F32),
            pltpu.VMEM((2, BANDS, SIDE), F32),
            pltpu.VMEM((2, ngrp, BANDS, SIDE), F32),
            pltpu.VMEM((2, BANDS, SIDE), F32),
            pltpu.VMEM((BANDS, SIDE), F32),
            pltpu.VMEM((3, CHUNKS, CH, SIDE), F32),
            pltpu.VMEM((8, 8, SIDE), F32),
            pltpu.VMEM((far, 8, SIDE), F32),
            pltpu.VMEM((16, SLOTS * BANDS), I32),
            pltpu.SMEM((16, SLOTS * BANDS), I32),
            dma((NSTAGE,)),
            dma((6,)),
            dma((CHUNKS,)),
            dma((CHUNKS, PIECES)),
            dma,
            dma((CHUNKS, PIECES)),
            dma((2, CHUNKS, PIECES)),
            dma((CHUNKS, PIECES)),
            dma((2, CHUNKS, PIECES)),
            dma((2, ngrp)),
            dma((2, ngrp)),
            dma((8,)),
            dma((8,)),
            dma((far,)),
            dma((far,)),
            dma,
            dma,
        ],
        compiler_params=pltpu.CompilerParams(
            collective_id=0, has_side_effects=True, vmem_limit_bytes=60 * 1024 * 1024
        ),
    )(
        start,
        momenta,
        observed.reshape(BANDS, SIDE),
        precision_obs.reshape(BANDS, SIDE),
        blocks.reshape(BANDS * SLOTS, SIDE, SIDE),
        block_cols.T,
        block_count.reshape(1, BANDS),
        block_count,
        step_size,
        trajectory.reshape(1, chains),
    )
    position, momentum, chees = pl.pallas_call(
        hand_over,
        out_shape=(
            jax.ShapeDtypeStruct((chains, CELLS), F32),
            jax.ShapeDtypeStruct((chains, CELLS), F32),
            jax.ShapeDtypeStruct((1, chains), F32),
        ),
        in_specs=[hbm, hbm, vmem],
        out_specs=(hbm, hbm, vmem),
        scratch_shapes=[pltpu.VMEM((2, chains, CELLS), F32), dma((2, STRIPS)), dma((2, STRIPS))],
    )(position, momentum, chees)
    return position, momentum, chees.reshape(chains)


def solution(mesh):
    placed = (
        P("grp", "rows"),
        P("grp", "rows"),
        P("rows"),
        P("rows"),
        P("rows", None, None, None),
        P("rows", None),
        P("rows"),
        P(),
        P("grp"),
    )
    return jax.shard_map(
        on_device,
        mesh=mesh,
        in_specs=placed,
        out_specs=(P("grp", "rows"), P("grp", "rows"), P("grp")),
        check_vma=False,
    )
```

```python
import functools

import jax
import jax.numpy as jnp
from jax import lax
from jax.experimental import pallas as pl
from jax.experimental.pallas import tpu as pltpu
from jax.sharding import PartitionSpec as P

F32 = jnp.float32
BF16 = jnp.bfloat16
I32 = jnp.int32
NN = (((1,), (0,)), ((), ()))

SIDE = 128
SLOTS = 4
OFF = SLOTS - 1
BANDS = 64
CELLS = BANDS * SIDE
EDGES = BANDS * OFF
CHUNKS = 2
CH = 32
PIECES = 4
PB = BANDS // PIECES
PE = EDGES // PIECES
LOAD = 4
NLOAD = BANDS // LOAD
NSTAGE = 4
STRIPS = 1


def dot(a, b):
    return lax.dot_general(a, b, NN, preferred_element_type=F32)


def split_rows(x):
    high = x.astype(BF16)
    low = (x - high.astype(F32)).astype(BF16)
    return jnp.concatenate([high, low], axis=0)


def split_lanes(x):
    high = x.astype(BF16)
    low = (x - high.astype(F32)).astype(BF16)
    return jnp.concatenate([high, low], axis=1)


def joined(p):
    return (p[:CH, :SIDE] + p[:CH, SIDE:]) + p[CH:, :SIDE]


def joined_both(p):
    return jnp.concatenate([joined(p[c * 2 * CH : (c + 1) * 2 * CH]) for c in range(CHUNKS)], axis=0)


def lanes(r):
    return pl.ds(pl.multiple_of(r * SIDE, SIDE), SIDE)


def edge_tables(cols_ref, count_ref, first, nblocks, table_ref):
    total = BANDS * SLOTS
    count = count_ref[...]
    sub = lax.broadcasted_iota(I32, (BANDS, BANDS), 0)
    lane = lax.broadcasted_iota(I32, (BANDS, BANDS), 1)
    row_id = lax.broadcasted_iota(I32, (1, BANDS), 1)
    col_id = lax.broadcasted_iota(I32, (BANDS, 1), 0)

    def column(row):
        return jnp.sum(jnp.where(sub == lane, row, 0), axis=1, keepdims=True)

    local, dest_col, key_row, key_col = [], [], [], []
    for s in range(1, SLOTS):
        d = cols_ref[s : s + 1, :] - first
        d = jnp.where(d < 0, d + nblocks, d)
        local.append(jnp.minimum(d, 2 * BANDS - 1))
        live = jnp.where(s < count, d, 0)
        key = (row_id // PB) * (1 << 20) + live * total + row_id * OFF + (s - 1)
        dest_col.append(column(live))
        key_row.append(key)
        key_col.append(column(key))
    place = lax.broadcasted_iota(I32, (BANDS, total), 1)
    edge = jnp.zeros((1, total), I32)
    band = jnp.zeros((1, total), I32)
    dest = jnp.zeros((1, total), I32)
    before = jnp.zeros((1, total), I32)

    def down(x):
        return jnp.sum(x, axis=0, keepdims=True)

    for s in range(OFF):
        rank = jnp.zeros((BANDS, 1), I32)
        for k in range(OFF):
            rank += jnp.sum(jnp.where(key_row[k] > key_col[s], 1, 0), axis=1, keepdims=True)
        here = rank == place
        edge += down(jnp.where(here, col_id * OFF + s, 0))
        band += down(jnp.where(here, col_id, 0))
        dest += down(jnp.where(here, dest_col[s], 0))
        before += down(jnp.where(rank + 1 == place, dest_col[s], 0))
    table_ref[0:1, :] = edge
    table_ref[1:2, :] = band
    table_ref[2:3, :] = jnp.where(dest == before, 1, 0)
    pad = jnp.zeros((1, total - BANDS), I32)
    for s in range(OFF):
        table_ref[3 + s : 4 + s, :] = jnp.concatenate([local[s], pad], axis=1)
    spot = lax.broadcasted_iota(I32, (PB, total), 1)
    spot = jnp.where(spot < SIDE, spot, spot - SIDE)
    side = lax.broadcasted_iota(I32, (1, total), 1)
    for q in range(PIECES):
        upto = jnp.zeros((1, total), I32)
        found = jnp.zeros((1, total), I32)
        for s in range(OFF):
            d = dest_col[s][q * PB : (q + 1) * PB, :]
            upto += down(jnp.where(d >= spot, 1, 0))
            found += down(jnp.where(d == spot, 1, 0))
        last = jnp.maximum(upto - 1, 0)
        table_ref[6 + q : 7 + q, :] = jnp.where(side < SIDE, last, jnp.minimum(found, 1))


def kernel(
    nrows,
    ngrp,
    chain_total,
    all_cells,
    start_hbm,
    momenta_hbm,
    observed_hbm,
    precision_hbm,
    blocks_hbm,
    cols_ref,
    count_ref,
    count_smem,
    step_smem,
    trajectory_ref,
    position_hbm,
    momentum_hbm,
    chees_ref,
    stage,
    flat,
    turned,
    v,
    m,
    split,
    u,
    sums,
    next_v,
    carried,
    obs,
    prec,
    cell_sums,
    cell_all,
    mean,
    mean_next,
    acc,
    part,
    part_y,
    table,
    smem,
    stage_sem,
    load_sem,
    out_sem,
    momentum_sem,
    table_sem,
    up_send,
    up_recv,
    dn_send,
    dn_recv,
    x_send,
    x_recv,
    a_send,
    a_recv,
    b_send,
    b_recv,
    mean_send,
    mean_recv,
):
    me = lax.axis_index("rows")
    grp = lax.axis_index("grp")
    up = lax.rem(me + nrows - 1, nrows)
    down = lax.rem(me + 1, nrows)
    near = 8
    far = nrows // near
    in_near = lax.rem(me, near)
    base = me - in_near
    in_far = me // near

    def near_peer(d):
        return base + lax.rem(in_near + d, near)

    def far_peer(d):
        return lax.rem(me + near * d, nrows)

    def piece_cells(p):
        return pl.ds(pl.multiple_of(p * (PB * SIDE), PB * SIDE), PB * SIDE)

    def load_v(c):
        return pltpu.make_async_copy(start_hbm.at[pl.ds(c * CH, CH)], v.at[c], load_sem.at[c])

    def load_m(c):
        return pltpu.make_async_copy(momenta_hbm.at[pl.ds(c * CH, CH)], m.at[c], load_sem.at[2 + c])

    load_obs = pltpu.make_async_copy(observed_hbm, obs, load_sem.at[4])
    load_prec = pltpu.make_async_copy(precision_hbm, prec, load_sem.at[5])

    def load_band(i):
        per = PB // LOAD
        return ((PIECES - 1 - i // per) * per + lax.rem(i, per)) * LOAD

    def load_blocks(i):
        slot = lax.rem(i, NSTAGE)
        rows = pl.ds(load_band(i) * SLOTS, LOAD * SLOTS)
        return pltpu.make_async_copy(blocks_hbm.at[rows], stage.at[slot], stage_sem.at[slot])

    def store_position(c):
        return pltpu.make_async_copy(v.at[c], position_hbm.at[pl.ds(c * CH, CH)], out_sem.at[c])

    def store_momentum(c, p):
        cells = piece_cells(p)
        return pltpu.make_async_copy(
            m.at[c, :, cells], momentum_hbm.at[pl.ds(c * CH, CH), cells], momentum_sem.at[c, p]
        )

    def send_up(g, c, p):
        par = lax.rem(g, 2)
        return pltpu.make_async_remote_copy(
            v.at[c, :, piece_cells(p)],
            next_v.at[par, c, :, piece_cells(p)],
            up_send.at[c, p],
            up_recv.at[par, c, p],
            device_id={"rows": up},
        )

    def send_down(g, c, p):
        par = lax.rem(g, 2)
        return pltpu.make_async_remote_copy(
            u.at[c, :, pl.ds(pl.multiple_of(CELLS + p * (PB * SIDE), PB * SIDE), PB * SIDE)],
            carried.at[par, c, :, piece_cells(p)],
            dn_send.at[c, p],
            dn_recv.at[par, c, p],
            device_id={"rows": down},
        )

    def send_sums(which, d):
        return pltpu.make_async_remote_copy(
            cell_sums.at[which],
            cell_all.at[which, grp],
            x_send.at[which, d],
            x_recv.at[which, grp],
            device_id={"grp": lax.rem(grp + d, ngrp)},
        )

    def take_sums(which, d):
        slot = lax.rem(grp + d, ngrp)
        return pltpu.make_async_remote_copy(
            cell_sums.at[which],
            cell_all.at[which, slot],
            x_send.at[which, d],
            x_recv.at[which, slot],
            device_id={"grp": slot},
        )

    send_mean = pltpu.make_async_remote_copy(
        mean.at[1], mean_next, mean_send, mean_recv, device_id={"rows": up}
    )

    for c in range(CHUNKS):
        load_v(c).start()
    for i in range(NSTAGE):
        load_blocks(i).start()
    load_obs.start()
    load_prec.start()

    barrier = pltpu.get_barrier_semaphore()
    for peer in (up, down):
        pl.semaphore_signal(barrier, inc=1, device_id={"rows": peer})
    for d in range(1, ngrp):
        pl.semaphore_signal(barrier, inc=1, device_id={"grp": lax.rem(grp + d, ngrp)})
    for d in range(1, near):
        pl.semaphore_signal(barrier, inc=1, device_id={"rows": near_peer(d)})
    for d in range(1, far):
        pl.semaphore_signal(barrier, inc=1, device_id={"rows": far_peer(d)})

    pl.semaphore_wait(barrier, 2 + (ngrp - 1) + (near - 1) + (far - 1))

    for c in range(CHUNKS):
        load_v(c).wait()
        for p in range(PIECES):
            send_up(0, c, p).start()

    edge_tables(cols_ref, count_ref, me * BANDS, nrows * BANDS, table)
    to_smem = pltpu.make_async_copy(table, smem, table_sem)
    to_smem.start()

    def first_cells(r, _):
        total = jnp.zeros((1, SIDE), F32)
        for c in range(CHUNKS):
            x = v[c, :, lanes(r)]
            total += jnp.sum(x, axis=0, keepdims=True)
            split[c, r] = split_rows(x)
        cell_sums[0, pl.ds(r, 1), :] = total
        return 0

    lax.fori_loop(0, BANDS, first_cells, 0, unroll=8)
    for d in range(1, ngrp):
        send_sums(0, d).start()

    def take_blocks(i, _):
        load_blocks(i).wait()
        slot = lax.rem(i, NSTAGE)
        for k in range(LOAD):
            r = load_band(i) + k
            count = count_smem[r]
            for s in range(SLOTS):
                b = stage[slot, k * SLOTS + s]
                if s >= 2:
                    b = jnp.where(s < count, b, 0.0)
                pair = split_lanes(b)
                if s == 0:
                    turned[r, 0:SIDE, :] = pair
                else:
                    flat[r * OFF + (s - 1)] = pair

        @pl.when(i + NSTAGE < NLOAD)
        def _():
            load_blocks(i + NSTAGE).start()

        return 0

    to_smem.wait()

    def spread_out(pairs, p):
        def found(r, i):
            x = sums[smem[6 + p, r], i * CH : (i + 1) * CH, :]
            return jnp.where(smem[6 + p, SIDE + r] != 0, x, 0.0)

        def fresh(j, _):
            r = p * PB + j
            for i, c in pairs:
                u[c, :, lanes(r)] = found(r, i)
            return 0

        def more(j, _):
            r = p * PB + j
            for i, c in pairs:
                u[c, :, lanes(r)] = u[c, :, lanes(r)] + found(r, i)
            return 0

        lax.fori_loop(0, PB, fresh, 0, unroll=8)

        @pl.when(p == PIECES - 1)
        def _():
            lax.fori_loop(PB, PB + BANDS, fresh, 0, unroll=8)

        @pl.when(p < PIECES - 1)
        def _():
            lax.fori_loop(PB, PB + BANDS, more, 0, unroll=8)

    def quarter(g, c, p):
        def edge(k, total):
            place = (PIECES - 1 - p) * PE + k
            term = joined(dot(split[c, smem[1, place]], flat[smem[0, place]]))
            total = jnp.where(smem[2, place] != 0, total, 0.0) + term
            sums[k, :CH, :] = total
            return total

        place = (PIECES - 1 - p) * PE
        total = joined(dot(split[c, smem[1, place]], flat[smem[0, place]]))
        sums[0, :CH, :] = total
        lax.fori_loop(1, PE, edge, total, unroll=PE - 1)
        spread_out(((0, c),), p)
        send_down(g, c, p).start()

    def first_quarter(q, _):
        p = PIECES - 1 - q
        per = NLOAD // PIECES
        lax.fori_loop(q * per, (q + 1) * per, take_blocks, 0)

        def edges(i, total):
            r = p * PB + i
            for s in range(OFF):
                place = q * PE + i * OFF + s
                band = smem[1, place]
                both = jnp.concatenate([split[c, band] for c in range(CHUNKS)], axis=0)
                term = joined_both(dot(both, flat[smem[0, place]]))
                keep = smem[2, place]
                if s == 0:
                    keep = jnp.where(i == 0, 0, keep)
                total = jnp.where(keep != 0, total, 0.0) + term
                sums[i * OFF + s] = total
                x = flat[r * OFF + s]
                turned[r, (s + 1) * SIDE : (s + 2) * SIDE, :] = jnp.concatenate(
                    [x[:, :SIDE].T, x[:, SIDE:].T], axis=1
                )
            return total

        lax.fori_loop(0, PB, edges, jnp.zeros((CHUNKS * CH, SIDE), F32), unroll=PB)
        spread_out(((0, 0),), p)
        send_down(0, 0, p).start()
        spread_out(((1, 1),), p)
        return 0

    lax.fori_loop(0, PIECES, first_quarter, 0)
    for c in range(CHUNKS):
        load_m(c).start()
    for p in reversed(range(PIECES)):
        send_down(0, 1, p).start()

    def means(which):
        for d in range(1, ngrp):
            take_sums(which, d).wait_recv()
        cell_all[which, grp] = cell_sums[which]
        total = cell_all[which, 0]
        for k in range(1, ngrp):
            total = total + cell_all[which, k]
        mean[which] = total / chain_total

    def spread(which):
        for c in range(CHUNKS):

            def add(r, total):
                x = v[c, :, lanes(r)] - mean[which, pl.ds(r, 1), :]
                return total + x * x

            acc[which, c] = lax.fori_loop(0, BANDS, add, jnp.zeros((CH, SIDE), F32), unroll=8)

    means(0)
    spread(0)
    for c in range(CHUNKS):
        load_m(c).wait()
    load_obs.wait()
    load_prec.wait()

    step = step_smem[0]

    def inner_here(c, p):
        def band(j, total):
            r = p * PB + j
            x = v[c, :, lanes(r)]
            pull = prec[pl.ds(r, 1), :] * (x - obs[pl.ds(r, 1), :])
            mom = m[c, :, lanes(r)] - (step / 2) * (u[c, :, lanes(r)] + pull)
            return total + (x - mean[1, pl.ds(r, 1), :]) * mom

        old = jnp.where(p == 0, 0.0, acc[2, c])
        acc[2, c] = lax.fori_loop(0, PB, band, old, unroll=8)

    def inner_ahead(c):
        def band(r, total):
            ahead = next_v[0, c, :, lanes(r)] - mean_next[pl.ds(r, 1), :]
            return total + ahead * u[c, :, lanes(BANDS + r)]

        total = lax.fori_loop(0, BANDS, band, jnp.zeros((CH, SIDE), F32), unroll=8)
        acc[2, c] = acc[2, c] - (step / 2) * total

    def upper(g, c):
        par = lax.rem(g, 2)

        def piece(p, _):
            send_up(g, c, p).wait_recv()

            def take(j, _):
                r = p * PB + j
                split[c, BANDS + r] = split_rows(next_v[par, c, :, lanes(r)])
                return 0

            lax.fori_loop(0, PB, take, 0, unroll=8)

            def row(j, _):
                r = p * PB + j
                rows = [split[c, r]] + [split[c, smem[3 + s, r]] for s in range(OFF)]
                term = joined(dot(jnp.concatenate(rows, axis=1), turned[r]))
                u[c, :, lanes(r)] = u[c, :, lanes(r)] + term
                return 0

            lax.fori_loop(0, PB, row, 0, unroll=PB)

            @pl.when((g == 2) & (c == 1))
            def _():
                inner_here(1, p)

            return 0

        lax.fori_loop(0, PIECES, piece, 0)

    def gradient(g, c, r):
        par = lax.rem(g, 2)
        x = v[c, :, lanes(r)]
        pull = prec[pl.ds(r, 1), :] * (x - obs[pl.ds(r, 1), :])
        return x, -(u[c, :, lanes(r)] + carried[par, c, :, lanes(r)]) - pull

    def move(g, c):
        kick = jnp.where(g == 0, step / 2, step)
        for p in range(PIECES):
            send_up(g, c, p).wait_send()

        def piece(q, _):
            p = PIECES - 1 - q
            send_down(g, c, p).wait_recv()

            def band(j, _):
                r = p * PB + j
                x, grad = gradient(g, c, r)
                mom = m[c, :, lanes(r)] + kick * grad
                m[c, :, lanes(r)] = mom
                x = x + step * mom
                v[c, :, lanes(r)] = x
                split[c, r] = split_rows(x)
                here = jnp.sum(x, axis=0, keepdims=True)
                old = jnp.where(c == 0, 0.0, cell_sums[1, pl.ds(r, 1), :])
                cell_sums[1, pl.ds(r, 1), :] = old + here
                return 0

            return lax.fori_loop(0, PB, band, 0, unroll=4)

        lax.fori_loop(0, PIECES, piece, 0)

    def finish(g, c):
        for p in range(PIECES):
            send_up(g, c, p).wait_send()

        def piece(q, _):
            p = PIECES - 1 - q
            send_down(g, c, p).wait_recv()

            def band(j, _):
                r = p * PB + j
                x, grad = gradient(g, c, r)
                m[c, :, lanes(r)] = m[c, :, lanes(r)] + (step / 2) * grad
                return 0

            lax.fori_loop(0, PB, band, 0, unroll=4)
            store_momentum(c, p).start()
            return 0

        lax.fori_loop(0, PIECES, piece, 0)

    def inner_late(c):
        def band(r, total):
            return total + (v[c, :, lanes(r)] - mean[1, pl.ds(r, 1), :]) * m[c, :, lanes(r)]

        acc[2, c] = lax.fori_loop(0, BANDS, band, jnp.zeros((CH, SIDE), F32), unroll=8)

    def near_copy(slot, d):
        return pltpu.make_async_remote_copy(
            part.at[in_near], part.at[slot], a_send.at[d], a_recv.at[slot], device_id={"rows": near_peer(d)}
        )

    def far_copy(slot, d):
        return pltpu.make_async_remote_copy(
            part_y.at[in_far], part_y.at[slot], b_send.at[d], b_recv.at[slot], device_id={"rows": far_peer(d)}
        )

    def start_sum():
        sub = lax.broadcasted_iota(I32, (CH, SIDE), 0)
        lane = lax.broadcasted_iota(I32, (CH, SIDE), 1)
        inner = jnp.zeros((1, SIDE), F32)
        change = jnp.zeros((1, SIDE), F32)
        for c in range(CHUNKS):
            here = lane == sub + c * CH
            column = jnp.sum(acc[2, c], axis=1, keepdims=True)
            inner += jnp.sum(jnp.where(here, column, 0.0), axis=0, keepdims=True)
            column = jnp.sum(acc[1, c], axis=1, keepdims=True) - jnp.sum(acc[0, c], axis=1, keepdims=True)
            change += jnp.sum(jnp.where(here, column, 0.0), axis=0, keepdims=True)
        own = jnp.concatenate([inner, change, jnp.zeros((6, SIDE), F32)], axis=0)

        part_y[in_far] = own
        for d in range(1, far):
            far_copy(in_far, d).start()
        for d in range(1, far):
            far_copy(lax.rem(in_far + d, far), d).wait_recv()
        total = part_y[0]
        for k in range(1, far):
            total = total + part_y[k]
        part[in_near] = total
        for d in range(1, near):
            near_copy(in_near, d).start()

    def end_sum():
        for d in range(1, near):
            near_copy(lax.rem(in_near + d, near), d).wait_recv()
        total = part[0]
        for k in range(1, near):
            total = total + part[k]
        chees_ref[...] = (
            trajectory_ref[...] * (total[1:2, : CHUNKS * CH] / all_cells) * (total[0:1, : CHUNKS * CH] / all_cells)
        )
        for d in range(1, near):
            near_copy(in_near, d).wait_send()
        for d in range(1, far):
            far_copy(in_far, d).wait_send()

    def stage_of(t, _):
        g = t // CHUNKS
        c = lax.rem(t, CHUNKS)
        upper(g, c)

        @pl.when(g < 2)
        def _():
            move(g, c)
            for p in range(PIECES):
                send_up(g + 1, c, p).start()

            @pl.when(g == 1)
            def _():
                store_position(c).start()

            @pl.when(t == 3)
            def _():
                for d in range(1, ngrp):
                    send_sums(1, d).start()

            for p in range(PIECES):
                send_down(g, c, p).wait_send()

            def again(q, _):
                quarter(g + 1, c, PIECES - 1 - q)
                return 0

            lax.fori_loop(0, PIECES, again, 0)

        @pl.when(t == 4)
        def _():
            means(1)
            send_mean.start()

        @pl.when(t == 5)
        def _():
            send_mean.wait_recv()
            inner_ahead(1)
            start_sum()

        @pl.when(g == 2)
        def _():
            finish(g, c)

        @pl.when(t == 4)
        def _():
            inner_late(0)
            spread(1)

        return 0

    lax.fori_loop(0, 3 * CHUNKS, stage_of, 0)
    end_sum()

    send_mean.wait_send()
    for which in range(2):
        for d in range(1, ngrp):
            send_sums(which, d).wait_send()
    for c in range(CHUNKS):
        for p in range(PIECES):
            send_down(2, c, p).wait_send()
        store_position(c).wait()
        for p in range(PIECES):
            store_momentum(c, p).wait()


def hand_over(position_ref, momentum_ref, chees_ref, position_out, momentum_out, chees_out, held, in_sem, out_sem):
    part = CHUNKS * CH // STRIPS
    reads, writes = [], []
    for k, (a, b) in enumerate(((position_ref, position_out), (momentum_ref, momentum_out))):
        for i in range(STRIPS):
            rows = pl.ds(i * part, part)
            reads.append(pltpu.make_async_copy(a.at[rows], held.at[k, rows], in_sem.at[k, i]))
            writes.append(pltpu.make_async_copy(held.at[k, rows], b.at[rows], out_sem.at[k, i]))
    for copy in reads:
        copy.start()
    chees_out[...] = chees_ref[...]
    for read, write in zip(reads, writes):
        read.wait()
        write.start()
    for copy in writes:
        copy.wait()


def on_device(start, momenta, observed, precision_obs, blocks, block_cols, block_count, step_size, trajectory):
    nrows = lax.axis_size("rows")
    ngrp = lax.axis_size("grp")
    far = nrows // 8
    hbm = pl.BlockSpec(memory_space=pltpu.HBM)
    vmem = pl.BlockSpec(memory_space=pltpu.VMEM)
    smem = pl.BlockSpec(memory_space=pltpu.SMEM)
    dma = pltpu.SemaphoreType.DMA
    chains = CHUNKS * CH
    position, momentum, chees = pl.pallas_call(
        functools.partial(kernel, nrows, ngrp, chains * ngrp, CELLS * nrows),
        out_shape=(
            jax.ShapeDtypeStruct((chains, CELLS), F32),
            jax.ShapeDtypeStruct((chains, CELLS), F32),
            jax.ShapeDtypeStruct((1, chains), F32),
        ),
        in_specs=[hbm, hbm, hbm, hbm, hbm, vmem, vmem, smem, smem, vmem],
        out_specs=(hbm, hbm, vmem),
        scratch_shapes=[
            pltpu.VMEM((NSTAGE, LOAD * SLOTS, SIDE, SIDE), F32),
            pltpu.VMEM((EDGES, SIDE, 2 * SIDE), BF16),
            pltpu.VMEM((BANDS, SLOTS * SIDE, 2 * SIDE), BF16),
            pltpu.VMEM((CHUNKS, CH, CELLS), F32),
            pltpu.VMEM((CHUNKS, CH, CELLS), F32),
            pltpu.VMEM((CHUNKS, 2 * BANDS, 2 * CH, SIDE), BF16),
            pltpu.VMEM((CHUNKS, CH, 2 * CELLS), F32),
            pltpu.VMEM((PE, CHUNKS * CH, SIDE), F32),
            pltpu.VMEM((2, CHUNKS, CH, CELLS), F32),
            pltpu.VMEM((2, CHUNKS, CH, CELLS), F32),
            pltpu.VMEM((BANDS, SIDE), F32),
            pltpu.VMEM((BANDS, SIDE), F32),
            pltpu.VMEM((2, BANDS, SIDE), F32),
            pltpu.VMEM((2, ngrp, BANDS, SIDE), F32),
            pltpu.VMEM((2, BANDS, SIDE), F32),
            pltpu.VMEM((BANDS, SIDE), F32),
            pltpu.VMEM((3, CHUNKS, CH, SIDE), F32),
            pltpu.VMEM((8, 8, SIDE), F32),
            pltpu.VMEM((far, 8, SIDE), F32),
            pltpu.VMEM((16, SLOTS * BANDS), I32),
            pltpu.SMEM((16, SLOTS * BANDS), I32),
            dma((NSTAGE,)),
            dma((6,)),
            dma((CHUNKS,)),
            dma((CHUNKS, PIECES)),
            dma,
            dma((CHUNKS, PIECES)),
            dma((2, CHUNKS, PIECES)),
            dma((CHUNKS, PIECES)),
            dma((2, CHUNKS, PIECES)),
            dma((2, ngrp)),
            dma((2, ngrp)),
            dma((8,)),
            dma((8,)),
            dma((far,)),
            dma((far,)),
            dma,
            dma,
        ],
        compiler_params=pltpu.CompilerParams(
            collective_id=0, has_side_effects=True, vmem_limit_bytes=60 * 1024 * 1024
        ),
    )(
        start,
        momenta,
        observed.reshape(BANDS, SIDE),
        precision_obs.reshape(BANDS, SIDE),
        blocks.reshape(BANDS * SLOTS, SIDE, SIDE),
        block_cols.T,
        block_count.reshape(1, BANDS),
        block_count,
        step_size,
        trajectory.reshape(1, chains),
    )
    position, momentum, chees = pl.pallas_call(
        hand_over,
        out_shape=(
            jax.ShapeDtypeStruct((chains, CELLS), F32),
            jax.ShapeDtypeStruct((chains, CELLS), F32),
            jax.ShapeDtypeStruct((1, chains), F32),
        ),
        in_specs=[hbm, hbm, vmem],
        out_specs=(hbm, hbm, vmem),
        scratch_shapes=[pltpu.VMEM((2, chains, CELLS), F32), dma((2, STRIPS)), dma((2, STRIPS))],
    )(position, momentum, chees)
    return position, momentum, chees.reshape(chains)


def solution(mesh):
    placed = (
        P("grp", "rows"),
        P("grp", "rows"),
        P("rows"),
        P("rows"),
        P("rows", None, None, None),
        P("rows", None),
        P("rows"),
        P(),
        P("grp"),
    )
    return jax.shard_map(
        on_device,
        mesh=mesh,
        in_specs=placed,
        out_specs=(P("grp", "rows"), P("grp", "rows"), P("grp")),
        check_vma=False,
    )
```

```python
import functools

import jax
import jax.numpy as jnp
from jax import lax
from jax.experimental import pallas as pl
from jax.experimental.pallas import tpu as pltpu
from jax.sharding import PartitionSpec as P

F32 = jnp.float32
BF16 = jnp.bfloat16
I32 = jnp.int32
NN = (((1,), (0,)), ((), ()))

SIDE = 128
SLOTS = 4
OFF = SLOTS - 1
BANDS = 64
CELLS = BANDS * SIDE
EDGES = BANDS * OFF
CHUNKS = 2
CH = 32
PIECES = 4
PB = BANDS // PIECES
PE = EDGES // PIECES
LOAD = 4
NLOAD = BANDS // LOAD
NSTAGE = 4
STRIPS = 2


def dot(a, b):
    return lax.dot_general(a, b, NN, preferred_element_type=F32)


def split_rows(x):
    high = x.astype(BF16)
    low = (x - high.astype(F32)).astype(BF16)
    return jnp.concatenate([high, low], axis=0)


def split_lanes(x):
    high = x.astype(BF16)
    low = (x - high.astype(F32)).astype(BF16)
    return jnp.concatenate([high, low], axis=1)


def joined(p):
    return (p[:CH, :SIDE] + p[:CH, SIDE:]) + p[CH:, :SIDE]


def joined_both(p):
    return jnp.concatenate([joined(p[c * 2 * CH : (c + 1) * 2 * CH]) for c in range(CHUNKS)], axis=0)


def lanes(r):
    return pl.ds(pl.multiple_of(r * SIDE, SIDE), SIDE)


def edge_tables(cols_ref, count_ref, first, nblocks, table_ref):
    total = BANDS * SLOTS
    count = count_ref[...]
    sub = lax.broadcasted_iota(I32, (BANDS, BANDS), 0)
    lane = lax.broadcasted_iota(I32, (BANDS, BANDS), 1)
    row_id = lax.broadcasted_iota(I32, (1, BANDS), 1)
    col_id = lax.broadcasted_iota(I32, (BANDS, 1), 0)

    def column(row):
        return jnp.sum(jnp.where(sub == lane, row, 0), axis=1, keepdims=True)

    local, dest_col, key_row, key_col = [], [], [], []
    for s in range(1, SLOTS):
        d = cols_ref[s : s + 1, :] - first
        d = jnp.where(d < 0, d + nblocks, d)
        local.append(jnp.minimum(d, 2 * BANDS - 1))
        live = jnp.where(s < count, d, 0)
        key = (row_id // PB) * (1 << 20) + live * total + row_id * OFF + (s - 1)
        dest_col.append(column(live))
        key_row.append(key)
        key_col.append(column(key))
    place = lax.broadcasted_iota(I32, (BANDS, total), 1)
    edge = jnp.zeros((1, total), I32)
    band = jnp.zeros((1, total), I32)
    dest = jnp.zeros((1, total), I32)
    before = jnp.zeros((1, total), I32)

    def down(x):
        return jnp.sum(x, axis=0, keepdims=True)

    for s in range(OFF):
        rank = jnp.zeros((BANDS, 1), I32)
        for k in range(OFF):
            rank += jnp.sum(jnp.where(key_row[k] > key_col[s], 1, 0), axis=1, keepdims=True)
        here = rank == place
        edge += down(jnp.where(here, col_id * OFF + s, 0))
        band += down(jnp.where(here, col_id, 0))
        dest += down(jnp.where(here, dest_col[s], 0))
        before += down(jnp.where(rank + 1 == place, dest_col[s], 0))
    table_ref[0:1, :] = edge
    table_ref[1:2, :] = band
    table_ref[2:3, :] = jnp.where(dest == before, 1, 0)
    pad = jnp.zeros((1, total - BANDS), I32)
    for s in range(OFF):
        table_ref[3 + s : 4 + s, :] = jnp.concatenate([local[s], pad], axis=1)
    spot = lax.broadcasted_iota(I32, (PB, total), 1)
    spot = jnp.where(spot < SIDE, spot, spot - SIDE)
    side = lax.broadcasted_iota(I32, (1, total), 1)
    for q in range(PIECES):
        upto = jnp.zeros((1, total), I32)
        found = jnp.zeros((1, total), I32)
        for s in range(OFF):
            d = dest_col[s][q * PB : (q + 1) * PB, :]
            upto += down(jnp.where(d >= spot, 1, 0))
            found += down(jnp.where(d == spot, 1, 0))
        last = jnp.maximum(upto - 1, 0)
        table_ref[6 + q : 7 + q, :] = jnp.where(side < SIDE, last, jnp.minimum(found, 1))


def kernel(
    nrows,
    ngrp,
    chain_total,
    all_cells,
    start_hbm,
    momenta_hbm,
    observed_hbm,
    precision_hbm,
    blocks_hbm,
    cols_ref,
    count_ref,
    count_smem,
    step_smem,
    trajectory_ref,
    position_hbm,
    momentum_hbm,
    chees_ref,
    stage,
    flat,
    turned,
    v,
    m,
    split,
    u,
    sums,
    next_v,
    carried,
    obs,
    prec,
    cell_sums,
    cell_all,
    mean,
    mean_next,
    acc,
    part,
    part_y,
    table,
    smem,
    stage_sem,
    load_sem,
    out_sem,
    momentum_sem,
    table_sem,
    up_send,
    up_recv,
    dn_send,
    dn_recv,
    x_send,
    x_recv,
    a_send,
    a_recv,
    b_send,
    b_recv,
    mean_send,
    mean_recv,
):
    me = lax.axis_index("rows")
    grp = lax.axis_index("grp")
    up = lax.rem(me + nrows - 1, nrows)
    down = lax.rem(me + 1, nrows)
    near = 8
    far = nrows // near
    in_near = lax.rem(me, near)
    base = me - in_near
    in_far = me // near

    def near_peer(d):
        return base + lax.rem(in_near + d, near)

    def far_peer(d):
        return lax.rem(me + near * d, nrows)

    def piece_cells(p):
        return pl.ds(pl.multiple_of(p * (PB * SIDE), PB * SIDE), PB * SIDE)

    def load_v(c):
        return pltpu.make_async_copy(start_hbm.at[pl.ds(c * CH, CH)], v.at[c], load_sem.at[c])

    def load_m(c):
        return pltpu.make_async_copy(momenta_hbm.at[pl.ds(c * CH, CH)], m.at[c], load_sem.at[2 + c])

    load_obs = pltpu.make_async_copy(observed_hbm, obs, load_sem.at[4])
    load_prec = pltpu.make_async_copy(precision_hbm, prec, load_sem.at[5])

    def load_band(i):
        per = PB // LOAD
        return ((PIECES - 1 - i // per) * per + lax.rem(i, per)) * LOAD

    def load_blocks(i):
        slot = lax.rem(i, NSTAGE)
        rows = pl.ds(load_band(i) * SLOTS, LOAD * SLOTS)
        return pltpu.make_async_copy(blocks_hbm.at[rows], stage.at[slot], stage_sem.at[slot])

    def store_position(c):
        return pltpu.make_async_copy(v.at[c], position_hbm.at[pl.ds(c * CH, CH)], out_sem.at[c])

    def store_momentum(c, p):
        cells = piece_cells(p)
        return pltpu.make_async_copy(
            m.at[c, :, cells], momentum_hbm.at[pl.ds(c * CH, CH), cells], momentum_sem.at[c, p]
        )

    def send_up(g, c, p):
        par = lax.rem(g, 2)
        return pltpu.make_async_remote_copy(
            v.at[c, :, piece_cells(p)],
            next_v.at[par, c, :, piece_cells(p)],
            up_send.at[c, p],
            up_recv.at[par, c, p],
            device_id={"rows": up},
        )

    def send_down(g, c, p):
        par = lax.rem(g, 2)
        return pltpu.make_async_remote_copy(
            u.at[c, :, pl.ds(pl.multiple_of(CELLS + p * (PB * SIDE), PB * SIDE), PB * SIDE)],
            carried.at[par, c, :, piece_cells(p)],
            dn_send.at[c, p],
            dn_recv.at[par, c, p],
            device_id={"rows": down},
        )

    def send_sums(which, d):
        return pltpu.make_async_remote_copy(
            cell_sums.at[which],
            cell_all.at[which, grp],
            x_send.at[which, d],
            x_recv.at[which, grp],
            device_id={"grp": lax.rem(grp + d, ngrp)},
        )

    def take_sums(which, d):
        slot = lax.rem(grp + d, ngrp)
        return pltpu.make_async_remote_copy(
            cell_sums.at[which],
            cell_all.at[which, slot],
            x_send.at[which, d],
            x_recv.at[which, slot],
            device_id={"grp": slot},
        )

    send_mean = pltpu.make_async_remote_copy(
        mean.at[1], mean_next, mean_send, mean_recv, device_id={"rows": up}
    )

    for c in range(CHUNKS):
        load_v(c).start()
    for i in range(NSTAGE):
        load_blocks(i).start()
    load_obs.start()
    load_prec.start()

    barrier = pltpu.get_barrier_semaphore()
    for peer in (up, down):
        pl.semaphore_signal(barrier, inc=1, device_id={"rows": peer})
    for d in range(1, ngrp):
        pl.semaphore_signal(barrier, inc=1, device_id={"grp": lax.rem(grp + d, ngrp)})
    for d in range(1, near):
        pl.semaphore_signal(barrier, inc=1, device_id={"rows": near_peer(d)})
    for d in range(1, far):
        pl.semaphore_signal(barrier, inc=1, device_id={"rows": far_peer(d)})

    pl.semaphore_wait(barrier, 2 + (ngrp - 1) + (near - 1) + (far - 1))

    for c in range(CHUNKS):
        load_v(c).wait()
        for p in range(PIECES):
            send_up(0, c, p).start()

    edge_tables(cols_ref, count_ref, me * BANDS, nrows * BANDS, table)
    to_smem = pltpu.make_async_copy(table, smem, table_sem)
    to_smem.start()

    def first_cells(r, _):
        total = jnp.zeros((1, SIDE), F32)
        for c in range(CHUNKS):
            x = v[c, :, lanes(r)]
            total += jnp.sum(x, axis=0, keepdims=True)
            split[c, r] = split_rows(x)
        cell_sums[0, pl.ds(r, 1), :] = total
        return 0

    lax.fori_loop(0, BANDS, first_cells, 0, unroll=8)
    for d in range(1, ngrp):
        send_sums(0, d).start()

    def take_blocks(i, _):
        load_blocks(i).wait()
        slot = lax.rem(i, NSTAGE)
        for k in range(LOAD):
            r = load_band(i) + k
            count = count_smem[r]
            for s in range(SLOTS):
                b = stage[slot, k * SLOTS + s]
                if s >= 2:
                    b = jnp.where(s < count, b, 0.0)
                pair = split_lanes(b)
                if s == 0:
                    turned[r, 0:SIDE, :] = pair
                else:
                    flat[r * OFF + (s - 1)] = pair

        @pl.when(i + NSTAGE < NLOAD)
        def _():
            load_blocks(i + NSTAGE).start()

        return 0

    to_smem.wait()

    def spread_out(pairs, p):
        def found(r, i):
            x = sums[smem[6 + p, r], i * CH : (i + 1) * CH, :]
            return jnp.where(smem[6 + p, SIDE + r] != 0, x, 0.0)

        def fresh(j, _):
            r = p * PB + j
            for i, c in pairs:
                u[c, :, lanes(r)] = found(r, i)
            return 0

        def more(j, _):
            r = p * PB + j
            for i, c in pairs:
                u[c, :, lanes(r)] = u[c, :, lanes(r)] + found(r, i)
            return 0

        lax.fori_loop(0, PB, fresh, 0, unroll=8)

        @pl.when(p == PIECES - 1)
        def _():
            lax.fori_loop(PB, PB + BANDS, fresh, 0, unroll=8)

        @pl.when(p < PIECES - 1)
        def _():
            lax.fori_loop(PB, PB + BANDS, more, 0, unroll=8)

    def quarter(g, c, p):
        def edge(k, total):
            place = (PIECES - 1 - p) * PE + k
            term = joined(dot(split[c, smem[1, place]], flat[smem[0, place]]))
            total = jnp.where(smem[2, place] != 0, total, 0.0) + term
            sums[k, :CH, :] = total
            return total

        place = (PIECES - 1 - p) * PE
        total = joined(dot(split[c, smem[1, place]], flat[smem[0, place]]))
        sums[0, :CH, :] = total
        lax.fori_loop(1, PE, edge, total, unroll=PE - 1)
        spread_out(((0, c),), p)
        send_down(g, c, p).start()

    def first_quarter(q, _):
        p = PIECES - 1 - q
        per = NLOAD // PIECES
        lax.fori_loop(q * per, (q + 1) * per, take_blocks, 0)

        def edges(i, total):
            r = p * PB + i
            for s in range(OFF):
                place = q * PE + i * OFF + s
                band = smem[1, place]
                both = jnp.concatenate([split[c, band] for c in range(CHUNKS)], axis=0)
                term = joined_both(dot(both, flat[smem[0, place]]))
                keep = smem[2, place]
                if s == 0:
                    keep = jnp.where(i == 0, 0, keep)
                total = jnp.where(keep != 0, total, 0.0) + term
                sums[i * OFF + s] = total
                x = flat[r * OFF + s]
                turned[r, (s + 1) * SIDE : (s + 2) * SIDE, :] = jnp.concatenate(
                    [x[:, :SIDE].T, x[:, SIDE:].T], axis=1
                )
            return total

        lax.fori_loop(0, PB, edges, jnp.zeros((CHUNKS * CH, SIDE), F32), unroll=PB)
        spread_out(((0, 0),), p)
        send_down(0, 0, p).start()
        spread_out(((1, 1),), p)
        return 0

    lax.fori_loop(0, PIECES, first_quarter, 0)
    for c in range(CHUNKS):
        load_m(c).start()
    for p in reversed(range(PIECES)):
        send_down(0, 1, p).start()

    def means(which):
        for d in range(1, ngrp):
            take_sums(which, d).wait_recv()
        cell_all[which, grp] = cell_sums[which]
        total = cell_all[which, 0]
        for k in range(1, ngrp):
            total = total + cell_all[which, k]
        mean[which] = total / chain_total

    def spread(which, c):
        def add(r, total):
            x = v[c, :, lanes(r)] - mean[which, pl.ds(r, 1), :]
            return total + x * x

        acc[which, c] = lax.fori_loop(0, BANDS, add, jnp.zeros((CH, SIDE), F32), unroll=8)

    means(0)
    for c in range(CHUNKS):
        load_m(c).wait()
    load_obs.wait()
    load_prec.wait()

    step = step_smem[0]

    def inner_here(c, p):
        def band(j, total):
            r = p * PB + j
            x = v[c, :, lanes(r)]
            pull = prec[pl.ds(r, 1), :] * (x - obs[pl.ds(r, 1), :])
            mom = m[c, :, lanes(r)] - (step / 2) * (u[c, :, lanes(r)] + pull)
            return total + (x - mean[1, pl.ds(r, 1), :]) * mom

        old = jnp.where(p == 0, 0.0, acc[2, c])
        acc[2, c] = lax.fori_loop(0, PB, band, old, unroll=8)

    def inner_ahead(c):
        def band(r, total):
            ahead = next_v[0, c, :, lanes(r)] - mean_next[pl.ds(r, 1), :]
            return total + ahead * u[c, :, lanes(BANDS + r)]

        total = lax.fori_loop(0, BANDS, band, jnp.zeros((CH, SIDE), F32), unroll=8)
        acc[2, c] = acc[2, c] - (step / 2) * total

    def upper(g, c):
        par = lax.rem(g, 2)

        def piece(p, _):
            send_up(g, c, p).wait_recv()

            def take(j, _):
                r = p * PB + j
                split[c, BANDS + r] = split_rows(next_v[par, c, :, lanes(r)])
                return 0

            lax.fori_loop(0, PB, take, 0, unroll=8)

            def row(j, _):
                r = p * PB + j
                rows = [split[c, r]] + [split[c, smem[3 + s, r]] for s in range(OFF)]
                term = joined(dot(jnp.concatenate(rows, axis=1), turned[r]))
                u[c, :, lanes(r)] = u[c, :, lanes(r)] + term
                return 0

            lax.fori_loop(0, PB, row, 0, unroll=PB)

            @pl.when((g == 2) & (c == 1))
            def _():
                inner_here(1, p)

            return 0

        lax.fori_loop(0, PIECES, piece, 0)

    def gradient(g, c, r):
        par = lax.rem(g, 2)
        x = v[c, :, lanes(r)]
        pull = prec[pl.ds(r, 1), :] * (x - obs[pl.ds(r, 1), :])
        return x, -(u[c, :, lanes(r)] + carried[par, c, :, lanes(r)]) - pull

    def move(g, c):
        kick = jnp.where(g == 0, step / 2, step)
        for p in range(PIECES):
            send_up(g, c, p).wait_send()

        def piece(q, _):
            p = PIECES - 1 - q
            send_down(g, c, p).wait_recv()

            def band(j, _):
                r = p * PB + j
                x, grad = gradient(g, c, r)
                mom = m[c, :, lanes(r)] + kick * grad
                m[c, :, lanes(r)] = mom
                x = x + step * mom
                v[c, :, lanes(r)] = x
                split[c, r] = split_rows(x)
                here = jnp.sum(x, axis=0, keepdims=True)
                old = jnp.where(c == 0, 0.0, cell_sums[1, pl.ds(r, 1), :])
                cell_sums[1, pl.ds(r, 1), :] = old + here
                return 0

            return lax.fori_loop(0, PB, band, 0, unroll=4)

        lax.fori_loop(0, PIECES, piece, 0)

    def finish(g, c):
        for p in range(PIECES):
            send_up(g, c, p).wait_send()

        def piece(q, _):
            p = PIECES - 1 - q
            send_down(g, c, p).wait_recv()

            def band(j, _):
                r = p * PB + j
                x, grad = gradient(g, c, r)
                m[c, :, lanes(r)] = m[c, :, lanes(r)] + (step / 2) * grad
                return 0

            lax.fori_loop(0, PB, band, 0, unroll=4)
            store_momentum(c, p).start()
            return 0

        lax.fori_loop(0, PIECES, piece, 0)

    def inner_late(c):
        def band(r, total):
            return total + (v[c, :, lanes(r)] - mean[1, pl.ds(r, 1), :]) * m[c, :, lanes(r)]

        acc[2, c] = lax.fori_loop(0, BANDS, band, jnp.zeros((CH, SIDE), F32), unroll=8)

    def near_copy(slot, d):
        return pltpu.make_async_remote_copy(
            part.at[in_near], part.at[slot], a_send.at[d], a_recv.at[slot], device_id={"rows": near_peer(d)}
        )

    def far_copy(slot, d):
        return pltpu.make_async_remote_copy(
            part_y.at[in_far], part_y.at[slot], b_send.at[d], b_recv.at[slot], device_id={"rows": far_peer(d)}
        )

    def start_sum():
        sub = lax.broadcasted_iota(I32, (CH, SIDE), 0)
        lane = lax.broadcasted_iota(I32, (CH, SIDE), 1)
        inner = jnp.zeros((1, SIDE), F32)
        change = jnp.zeros((1, SIDE), F32)
        for c in range(CHUNKS):
            here = lane == sub + c * CH
            column = jnp.sum(acc[2, c], axis=1, keepdims=True)
            inner += jnp.sum(jnp.where(here, column, 0.0), axis=0, keepdims=True)
            column = jnp.sum(acc[1, c], axis=1, keepdims=True) - jnp.sum(acc[0, c], axis=1, keepdims=True)
            change += jnp.sum(jnp.where(here, column, 0.0), axis=0, keepdims=True)
        own = jnp.concatenate([inner, change, jnp.zeros((6, SIDE), F32)], axis=0)

        part_y[in_far] = own
        for d in range(1, far):
            far_copy(in_far, d).start()
        for d in range(1, far):
            far_copy(lax.rem(in_far + d, far), d).wait_recv()
        total = part_y[0]
        for k in range(1, far):
            total = total + part_y[k]
        part[in_near] = total
        for d in range(1, near):
            near_copy(in_near, d).start()

    def end_sum():
        for d in range(1, near):
            near_copy(lax.rem(in_near + d, near), d).wait_recv()
        total = part[0]
        for k in range(1, near):
            total = total + part[k]
        chees_ref[...] = (
            trajectory_ref[...] * (total[1:2, : CHUNKS * CH] / all_cells) * (total[0:1, : CHUNKS * CH] / all_cells)
        )
        for d in range(1, near):
            near_copy(in_near, d).wait_send()
        for d in range(1, far):
            far_copy(in_far, d).wait_send()

    def stage_of(t, _):
        g = t // CHUNKS
        c = lax.rem(t, CHUNKS)
        @pl.when(g == 0)
        def _():
            spread(0, c)

        upper(g, c)

        @pl.when(g < 2)
        def _():
            move(g, c)
            for p in range(PIECES):
                send_up(g + 1, c, p).start()

            @pl.when(g == 1)
            def _():
                store_position(c).start()

            @pl.when(t == 3)
            def _():
                for d in range(1, ngrp):
                    send_sums(1, d).start()

            for p in range(PIECES):
                send_down(g, c, p).wait_send()

            def again(q, _):
                quarter(g + 1, c, PIECES - 1 - q)
                return 0

            lax.fori_loop(0, PIECES, again, 0)

        @pl.when(t == 4)
        def _():
            means(1)
            send_mean.start()

        @pl.when(t == 5)
        def _():
            send_mean.wait_recv()
            inner_ahead(1)
            start_sum()

        @pl.when(g == 2)
        def _():
            finish(g, c)

        @pl.when(t == 4)
        def _():
            inner_late(0)
            for k in range(CHUNKS):
                spread(1, k)

        return 0

    lax.fori_loop(0, 3 * CHUNKS, stage_of, 0)
    end_sum()

    send_mean.wait_send()
    for which in range(2):
        for d in range(1, ngrp):
            send_sums(which, d).wait_send()
    for c in range(CHUNKS):
        for p in range(PIECES):
            send_down(2, c, p).wait_send()
        store_position(c).wait()
        for p in range(PIECES):
            store_momentum(c, p).wait()


def hand_over(position_ref, momentum_ref, chees_ref, position_out, momentum_out, chees_out, held, in_sem, out_sem):
    part = CHUNKS * CH // STRIPS
    reads, writes = [], []
    for k, (a, b) in enumerate(((position_ref, position_out), (momentum_ref, momentum_out))):
        for i in range(STRIPS):
            rows = pl.ds(i * part, part)
            reads.append(pltpu.make_async_copy(a.at[rows], held.at[k, rows], in_sem.at[k, i]))
            writes.append(pltpu.make_async_copy(held.at[k, rows], b.at[rows], out_sem.at[k, i]))
    for copy in reads:
        copy.start()
    chees_out[...] = chees_ref[...]
    for read, write in zip(reads, writes):
        read.wait()
        write.start()
    for copy in writes:
        copy.wait()


def on_device(start, momenta, observed, precision_obs, blocks, block_cols, block_count, step_size, trajectory):
    nrows = lax.axis_size("rows")
    ngrp = lax.axis_size("grp")
    far = nrows // 8
    hbm = pl.BlockSpec(memory_space=pltpu.HBM)
    vmem = pl.BlockSpec(memory_space=pltpu.VMEM)
    smem = pl.BlockSpec(memory_space=pltpu.SMEM)
    dma = pltpu.SemaphoreType.DMA
    chains = CHUNKS * CH
    position, momentum, chees = pl.pallas_call(
        functools.partial(kernel, nrows, ngrp, chains * ngrp, CELLS * nrows),
        out_shape=(
            jax.ShapeDtypeStruct((chains, CELLS), F32),
            jax.ShapeDtypeStruct((chains, CELLS), F32),
            jax.ShapeDtypeStruct((1, chains), F32),
        ),
        in_specs=[hbm, hbm, hbm, hbm, hbm, vmem, vmem, smem, smem, vmem],
        out_specs=(hbm, hbm, vmem),
        scratch_shapes=[
            pltpu.VMEM((NSTAGE, LOAD * SLOTS, SIDE, SIDE), F32),
            pltpu.VMEM((EDGES, SIDE, 2 * SIDE), BF16),
            pltpu.VMEM((BANDS, SLOTS * SIDE, 2 * SIDE), BF16),
            pltpu.VMEM((CHUNKS, CH, CELLS), F32),
            pltpu.VMEM((CHUNKS, CH, CELLS), F32),
            pltpu.VMEM((CHUNKS, 2 * BANDS, 2 * CH, SIDE), BF16),
            pltpu.VMEM((CHUNKS, CH, 2 * CELLS), F32),
            pltpu.VMEM((PE, CHUNKS * CH, SIDE), F32),
            pltpu.VMEM((2, CHUNKS, CH, CELLS), F32),
            pltpu.VMEM((2, CHUNKS, CH, CELLS), F32),
            pltpu.VMEM((BANDS, SIDE), F32),
            pltpu.VMEM((BANDS, SIDE), F32),
            pltpu.VMEM((2, BANDS, SIDE), F32),
            pltpu.VMEM((2, ngrp, BANDS, SIDE), F32),
            pltpu.VMEM((2, BANDS, SIDE), F32),
            pltpu.VMEM((BANDS, SIDE), F32),
            pltpu.VMEM((3, CHUNKS, CH, SIDE), F32),
            pltpu.VMEM((8, 8, SIDE), F32),
            pltpu.VMEM((far, 8, SIDE), F32),
            pltpu.VMEM((16, SLOTS * BANDS), I32),
            pltpu.SMEM((16, SLOTS * BANDS), I32),
            dma((NSTAGE,)),
            dma((6,)),
            dma((CHUNKS,)),
            dma((CHUNKS, PIECES)),
            dma,
            dma((CHUNKS, PIECES)),
            dma((2, CHUNKS, PIECES)),
            dma((CHUNKS, PIECES)),
            dma((2, CHUNKS, PIECES)),
            dma((2, ngrp)),
            dma((2, ngrp)),
            dma((8,)),
            dma((8,)),
            dma((far,)),
            dma((far,)),
            dma,
            dma,
        ],
        compiler_params=pltpu.CompilerParams(
            collective_id=0, has_side_effects=True, vmem_limit_bytes=60 * 1024 * 1024
        ),
    )(
        start,
        momenta,
        observed.reshape(BANDS, SIDE),
        precision_obs.reshape(BANDS, SIDE),
        blocks.reshape(BANDS * SLOTS, SIDE, SIDE),
        block_cols.T,
        block_count.reshape(1, BANDS),
        block_count,
        step_size,
        trajectory.reshape(1, chains),
    )
    position, momentum, chees = pl.pallas_call(
        hand_over,
        out_shape=(
            jax.ShapeDtypeStruct((chains, CELLS), F32),
            jax.ShapeDtypeStruct((chains, CELLS), F32),
            jax.ShapeDtypeStruct((1, chains), F32),
        ),
        in_specs=[hbm, hbm, vmem],
        out_specs=(hbm, hbm, vmem),
        scratch_shapes=[pltpu.VMEM((2, chains, CELLS), F32), dma((2, STRIPS)), dma((2, STRIPS))],
    )(position, momentum, chees)
    return position, momentum, chees.reshape(chains)


def solution(mesh):
    placed = (
        P("grp", "rows"),
        P("grp", "rows"),
        P("rows"),
        P("rows"),
        P("rows", None, None, None),
        P("rows", None),
        P("rows"),
        P(),
        P("grp"),
    )
    return jax.shard_map(
        on_device,
        mesh=mesh,
        in_specs=placed,
        out_specs=(P("grp", "rows"), P("grp", "rows"), P("grp")),
        check_vma=False,
    )
```
